32 devices in a mesh: img: 4 (over y, x), cls: 8 (over z, core).
Axes of the slice: x: 2, y: 2, z: 4, core: 2. Of those that a mesh axis runs over, the one named last changes fastest.
Arguments:
- images: bfloat16 [3072, 256, 256], P(('img', 'cls')), may hold values from -6 to 6
- ctf_table: float32 [16, 128, 256], replicated, may hold values from -1 to 1
- defocus_bin: int32 [3072], P(('img', 'cls')), may hold values from 0 to 15
- projections: bfloat16 [8, 8, 128, 256], P('cls'), may hold values from -6 to 6
- best_class: int32 [3072, 1], P(('img', 'cls')), may hold values from 0 to 7; in each aligned block of 96 rows (0 to 95, 96 to 191, ...) at most 36 rows name the same one
- best_orient: int32 [3072], P(('img', 'cls')), may hold values from 0 to 7
- slice_slots: int32 [8, 128], replicated, may hold values from 0 to 511
- slot_weight: float32 [8, 128], replicated, may hold values from 0.25 to 1
Outputs:
- best_score: float32 [3072], P(('img', 'cls'))
- data_volume: float32 [8, 512, 256], P('cls', 'img')
- weight_volume: float32 [8, 512, 256], P('cls', 'img')
The draws below stay inside these ranges and needn't reach their ends.
Inputs may be any that keep to these rules, and one draw needn't show every extreme that they name: `best_class`: among the 96 images of one device (aligned blocks of rows), at most 36 name the same class, a bound that some blocks reach.
All inputs are finite; a program needn't handle non-finite values.
Results may differ from the reference program's by a relative error of at most 0.0052.
Values may be sent and summed in bfloat16 or wider, within the bound.
No kernel may reach another device: no remote copies, remote signals or barrier semaphores. Data moves between devices by JAX's collectives and lax.ppermute only.
A program may use at most 192 MiB of HBM per device.

```python
import math
import jax
import jax.numpy as jnp
import numpy as np
from jax import lax

PIX = 256
ROWS = 128
ORI = 8
CLS = 8
IMG_DEV = 96
IMAGES = 3072
CAP = 36
BINS = 16
SLOTS = 512


def place_ends(drawn, rng, smallest, high):
    longest = drawn.shape.index(max(drawn.shape))
    spots = []
    for shift in (0, 1):
        where = [jax.random.randint(jax.random.fold_in(rng, axis), (), 0, length) for axis, length in enumerate(drawn.shape)]
        where[longest] = (where[longest] + shift) % drawn.shape[longest]
        spots.append(tuple(where))
    return drawn.at[spots[0]].set(smallest).at[spots[1]].set(high)


def block_levels(own_key, shape, split, least, high):
    level, own = 1.0, jax.random.fold_in(own_key, 6)
    for dim, shards_of in split:
        draws = jnp.exp(jax.random.uniform(jax.random.fold_in(own, dim), (shards_of,), jnp.float32, least / len(split), high / len(split)))
        level = level * jnp.repeat(draws, shape[dim] // shards_of).reshape([-1 if axis == dim else 1 for axis in range(len(shape))])
    return level


def assign_block(own_key, own, number, rows, amount, top, bound, lean):
    order = jax.random.permutation(own_key, amount)
    heavy_load, ordinary = shares(amount, rows * top, bound, lean, True), shares(amount, rows * top, bound, lean, False)
    places = jnp.arange(amount)

    def named(sizes, turn):
        used = int((sizes > 0).sum())
        fixed = max(1, used // 4)
        shifted = fixed + (places - fixed + turn * (used - fixed)) % max(1, amount - fixed)
        return jnp.zeros((amount,), jnp.int32).at[order[jnp.where(places < fixed, places, shifted)]].set(jnp.asarray(sizes, jnp.int32))

    sizes = jnp.where(number % 4 == 0, named(heavy_load, number // 4), named(ordinary, number - number // 4 - 1))
    mixed = jax.random.permutation(jax.random.fold_in(own, 3), amount)
    source_of, taker = mixed[0:amount // 2 * 2:2], mixed[1:amount // 2 * 2:2]
    slack = jnp.minimum(sizes[source_of] - 1, bound - sizes[taker]) // 2
    slack = jnp.where((source_of == order[0]) | (taker == order[0]) | (sizes[taker] == 0), 0, jnp.maximum(slack, 0))
    shifted = jax.random.randint(jax.random.fold_in(own, 4), (amount // 2,), 0, 1 << 20) % (slack + 1)
    sizes = sizes.at[source_of].add(-shifted).at[taker].add(shifted)
    items = jnp.searchsorted(jnp.cumsum(sizes), jnp.arange(rows * top), side="right").astype(jnp.int32)
    grid = items.reshape(top, rows).T
    grid = grid[jax.random.permutation(jax.random.fold_in(own, 1), rows)]
    turn = jax.random.randint(jax.random.fold_in(own, 2), (rows, 1), 0, top)
    return jnp.take_along_axis(grid, (jnp.arange(top)[None, :] + turn) % top, axis=1)


def shares(number_of, total, bound, lean, full):
    weights = [(1 << 20) // math.isqrt(standing ** lean) + 1 for standing in range(1, number_of + 1)]
    largest = bound if full else min(bound, max(-(-total // number_of), total * weights[0] // sum(weights)))
    least = 1 if total - largest >= number_of - 1 else 0
    given, rest = [largest] + [least] * (number_of - 1), total - largest - least * (number_of - 1)
    while rest > 0:
        candidates = [i for i in range(1, number_of) if given[i] < largest] or [i for i in range(1, number_of) if given[i] < bound]
        whole, budget = sum([weights[i] for i in candidates]), rest
        for i in candidates:
            extra = min(bound - given[i], max(1, budget * weights[i] // whole), rest)
            given[i] = given[i] + extra
            rest = rest - extra
    return np.array(given)


def bell_draw(own_key, dims, scale, most, shards=(), kind=jnp.bfloat16):
    values = jax.random.normal(own_key, dims, jnp.float32) * scale
    if len(shards) > 0:
        values = block_levels(own_key, dims, shards, -0.22, 0.18) * values
    return jnp.clip(values, min=-most, max=most).astype(kind)


def setup_inputs(seed: int = 0) -> dict:
    streams_of = jax.random.split(jax.random.key(seed), 9)
    images = bell_draw(streams_of[0], (IMAGES, PIX, PIX), 1.0, 6.0, ((0, 32),))
    ctf_table = jnp.clip(jax.random.uniform(streams_of[1], (BINS, ROWS, PIX), jnp.float32, -1.0, 1.0), -1.0, 1.0)
    defocus_bin = place_ends(jax.random.randint(streams_of[2], (IMAGES,), 0, BINS), jax.random.fold_in(streams_of[2], 1), 0, BINS - 1).astype(jnp.int32)
    projections = bell_draw(streams_of[3], (CLS, ORI, ROWS, PIX), 1.0, 6.0, ((0, 8),))
    best_class_keys = jax.random.split(jax.random.fold_in(streams_of[4], 1), IMAGES // IMG_DEV)
    best_class_turns = jax.random.permutation(jax.random.fold_in(streams_of[4], 3), IMAGES // IMG_DEV)
    best_class = jax.vmap(lambda own, number: assign_block(jax.random.fold_in(streams_of[4], 2), own, number, IMG_DEV, CLS, 1, CAP, 2))(best_class_keys, best_class_turns).reshape((IMAGES, 1))
    best_orient = place_ends(jax.random.randint(streams_of[5], (IMAGES,), 0, ORI), jax.random.fold_in(streams_of[5], 1), 0, ORI - 1).astype(jnp.int32)
    slice_slots = place_ends(jax.random.randint(streams_of[6], (ORI, ROWS), 0, SLOTS), jax.random.fold_in(streams_of[6], 1), 0, SLOTS - 1).astype(jnp.int32)
    slot_weight = jnp.clip(jax.random.uniform(streams_of[7], (ORI, ROWS), jnp.float32, 0.25, 1.0), 0.25, 1.0)
    return {"images": images, "ctf_table": ctf_table, "defocus_bin": defocus_bin, "projections": projections, "best_class": best_class, "best_orient": best_orient, "slice_slots": slice_slots, "slot_weight": slot_weight}


def dft_tables(pixels):
    half_side = pixels // 2
    position = jnp.arange(pixels, dtype=jnp.int32)
    columns_freq = jnp.arange(half_side, dtype=jnp.int32)
    rows_freq = jnp.arange(half_side, dtype=jnp.int32) - half_side // 2
    norm_factor = 1.0 / math.sqrt(pixels)
    phase_cols = position[:, None] * columns_freq[None, :] % pixels
    angle_cols = phase_cols.astype(jnp.float32) * (2.0 * math.pi / pixels)
    col_table = (jnp.concatenate([jnp.cos(angle_cols), -jnp.sin(angle_cols)], axis=1) * norm_factor).astype(jnp.bfloat16)
    phase_rows = rows_freq[:, None] * position[None, :] % pixels
    angle_rows = phase_rows.astype(jnp.float32) * (2.0 * math.pi / pixels)
    cos_rows = (jnp.cos(angle_rows) * norm_factor).astype(jnp.bfloat16)
    sin_rows = (jnp.sin(angle_rows) * norm_factor).astype(jnp.bfloat16)
    return (col_table, cos_rows, sin_rows)

def spectrum_ref(image_block, tables):
    col_table, cos_rows, sin_rows = tables
    number, pixels = (image_block.shape[0], image_block.shape[1])
    half_side = pixels // 2
    section_one = jnp.dot(image_block.reshape(number * pixels, pixels), col_table, preferred_element_type=jnp.float32)
    section_one = section_one.astype(jnp.bfloat16).reshape(number, pixels, pixels).astype(jnp.float32)
    along_cos = jnp.einsum('jy,nyl->njl', cos_rows.astype(jnp.float32), section_one, precision=lax.Precision.HIGHEST)
    along_sin = jnp.einsum('jy,nyl->njl', sin_rows.astype(jnp.float32), section_one, precision=lax.Precision.HIGHEST)
    real_part = along_cos[:, :, :half_side] + along_sin[:, :, half_side:]
    imag_part = along_cos[:, :, half_side:] - along_sin[:, :, :half_side]
    return jnp.concatenate([real_part, imag_part], axis=2)

def reference(images, ctf_table, defocus_bin, projections, best_class, best_orient, slice_slots, slot_weight):
    tables = dft_tables(PIX)
    feature = ROWS * PIX
    blocks_total = IMAGES // IMG_DEV
    pair_total = CLS * ORI
    panel_rows = projections.reshape(pair_total, feature)
    ctf_flat = ctf_table.reshape(BINS, feature)
    class_ids = best_class[:, 0]

    def one_block(running, inputs):
        image_block, bin_block, class_block, orient_block = inputs
        spectrum = spectrum_ref(image_block, tables).reshape(IMG_DEV, feature)
        weighted = (spectrum * ctf_flat[bin_block]).astype(jnp.bfloat16)
        scores = jnp.dot(weighted, panel_rows.T, preferred_element_type=jnp.float32) * (1.0 / math.sqrt(feature))
        best_rows = lax.optimization_barrier(jnp.max(scores, axis=1))
        pair_key = class_block * ORI + orient_block
        pair_hot = (pair_key[:, None] == jnp.arange(pair_total, dtype=jnp.int32)[None, :]).astype(jnp.bfloat16)
        running = running + jnp.dot(pair_hot.T, weighted, preferred_element_type=jnp.float32)
        return (running, best_rows)
    scanned = (images.reshape(blocks_total, IMG_DEV, PIX, PIX), defocus_bin.reshape(blocks_total, IMG_DEV), class_ids.reshape(blocks_total, IMG_DEV), best_orient.reshape(blocks_total, IMG_DEV))
    orient_sums, best_rows = lax.scan(one_block, jnp.zeros((pair_total, feature), jnp.float32), scanned)
    best_score = best_rows.reshape(IMAGES)
    tally_key = (class_ids * ORI + best_orient) * BINS + defocus_bin
    tallies = jnp.zeros((CLS * ORI * BINS,), jnp.float32).at[tally_key].add(1.0).reshape(CLS, ORI, BINS)
    power_table = (ctf_table * ctf_table).reshape(BINS, feature)
    ctf_power = jnp.einsum('cob,bk->cok', tallies, power_table, precision=lax.Precision.HIGHEST)
    target = jnp.arange(SLOTS, dtype=jnp.int32)
    matrix = jnp.where(slice_slots.reshape(-1)[None, :] == target[:, None], slot_weight.reshape(-1)[None, :], jnp.zeros((), jnp.float32))
    data_volume = jnp.einsum('sq,cql->csl', matrix, orient_sums.reshape(CLS, ORI * ROWS, PIX), precision=lax.Precision.HIGHEST)
    weight_volume = jnp.einsum('sq,cql->csl', matrix, ctf_power.reshape(CLS, ORI * ROWS, PIX), precision=lax.Precision.HIGHEST)
    return (best_score, data_volume, weight_volume)
```

```python
import functools
import math

import jax
import jax.numpy as jnp
import numpy as np
from jax import lax
from jax.experimental import pallas as pl
from jax.experimental.pallas import tpu as pltpu
from jax.sharding import PartitionSpec as P

SLOTS = 512
BLOCK = 16


def dft_tables(pixels):
    half = pixels // 2
    position = np.arange(pixels)
    norm = 1.0 / math.sqrt(pixels)
    angle_cols = (position[:, None] * np.arange(half)[None, :] % pixels) * (2.0 * math.pi / pixels)
    col_table = np.concatenate([np.cos(angle_cols), -np.sin(angle_cols)], axis=1) * norm
    angle_rows = ((np.arange(half) - half // 2)[:, None] * position[None, :] % pixels) * (
        2.0 * math.pi / pixels
    )
    row_table = np.concatenate([np.cos(angle_rows), np.sin(angle_rows)], axis=0) * norm
    to_bf = lambda t: jnp.asarray(t.astype(np.float32), jnp.bfloat16)
    return to_bf(col_table), to_bf(row_table)


def front_kernel(
    blocks, pair_ref, bin_ref, core_ref, img_ref, col_ref, row_ref, ctf_ref, slot_ref, wt_ref,
    w2_ref, keep_ref, send_ref, acc, wscr, hot, hi_scr, lo_scr,
):
    step = pl.program_id(0)
    half = col_ref.shape[0] // 2
    orients = wt_ref.shape[1]
    rows = wt_ref.shape[0]
    number = img_ref.shape[0]

    @pl.when(step == 0)
    def _():
        acc[...] = jnp.zeros_like(acc)
        slots = lax.broadcasted_iota(jnp.int32, hot.shape, 0)
        hot[...] = jnp.where(slots == slot_ref[...], 1.0, 0.0).astype(jnp.bfloat16)

    @pl.when(step < blocks)
    def _():
        for i in range(number):
            one = jnp.dot(img_ref[i], col_ref[...], preferred_element_type=jnp.float32)
            both = jnp.dot(
                row_ref[...], one.astype(jnp.bfloat16), preferred_element_type=jnp.float32
            )
            index = step * number + i
            which_bin, which_pair = bin_ref[index], pair_ref[index]
            real = both[:rows, :half] + both[rows:, half:]
            imag = both[:rows, half:] - both[rows:, :half]
            for part, spec in enumerate((real, imag)):
                lanes = pl.ds(part * half, half)
                weighted = (spec * ctf_ref[which_bin, :, lanes]).astype(jnp.bfloat16)
                weighted = weighted.astype(jnp.float32)
                acc[which_pair, :, lanes] += weighted
                wscr[part, pl.ds(i * rows, rows), :] = weighted
        for j in range(rows):
            w2_ref[j] = jnp.concatenate(
                [
                    wscr[part, pl.ds(j, number, stride=rows), :]
                    for part in range(2)
                ],
                axis=1,
            ).astype(jnp.bfloat16)

    @pl.when(step >= blocks)
    def _():
        z = step - blocks
        core = core_ref[0]
        for part, which in enumerate((2 * z + core, 2 * z + 1 - core)):
            for o in range(orients):
                value = acc[which * orients + o] * wt_ref[:, o : o + 1]
                high = value.astype(jnp.bfloat16)
                low = (value - high.astype(jnp.float32)).astype(jnp.bfloat16)
                where = (pl.ds(o * rows, rows), pl.ds(part * 2 * half, 2 * half))
                hi_scr[where] = high
                lo_scr[where] = low
        slab = jnp.dot(hot[...], hi_scr[...], preferred_element_type=jnp.float32) + jnp.dot(
            hot[...], lo_scr[...], preferred_element_type=jnp.float32
        )
        keep_ref[0] = slab[:, : 2 * half]
        send_ref[0] = slab[:, 2 * half :].astype(jnp.bfloat16)


def front(images, ctf_table, pair, bins, core, slots_row, weight_cols, classes):
    number, pixels = images.shape[0], images.shape[1]
    bin_count, rows = ctf_table.shape[0], ctf_table.shape[1]
    orients = weight_cols.shape[1]
    col_table, row_table = dft_tables(pixels)
    blocks, groups = number // BLOCK, classes // 2
    at_block = lambda i: jnp.minimum(i, blocks - 1)
    at_group = lambda i: jnp.maximum(i - blocks, 0)
    whole = lambda shape: pl.BlockSpec(
        shape, lambda i, *_: (0,) * len(shape), pipeline_mode=pl.Buffered(1)
    )
    return pl.pallas_call(
        functools.partial(front_kernel, blocks),
        grid_spec=pltpu.PrefetchScalarGridSpec(
            num_scalar_prefetch=3,
            grid=(blocks + groups,),
            in_specs=[
                pl.BlockSpec((BLOCK, pixels, pixels), lambda i, *_: (at_block(i), 0, 0)),
                whole((pixels, pixels)),
                whole((pixels, pixels)),
                whole((bin_count, rows, pixels)),
                whole((1, orients * rows)),
                whole((rows, orients)),
            ],
            out_specs=[
                pl.BlockSpec((rows, BLOCK, pixels), lambda i, *_: (0, at_block(i), 0)),
                pl.BlockSpec((1, SLOTS, pixels), lambda i, *_: (at_group(i), 0, 0)),
                pl.BlockSpec((1, SLOTS, pixels), lambda i, *_: (at_group(i), 0, 0)),
            ],
            scratch_shapes=[
                pltpu.VMEM((classes * orients, rows, pixels), jnp.float32),
                pltpu.VMEM((2, BLOCK * rows, pixels // 2), jnp.float32),
                pltpu.VMEM((SLOTS, orients * rows), jnp.bfloat16),
                pltpu.VMEM((orients * rows, 2 * pixels), jnp.bfloat16),
                pltpu.VMEM((orients * rows, 2 * pixels), jnp.bfloat16),
            ],
        ),
        out_shape=[
            jax.ShapeDtypeStruct((rows, number, pixels), jnp.bfloat16),
            jax.ShapeDtypeStruct((groups, SLOTS, pixels), jnp.float32),
            jax.ShapeDtypeStruct((groups, SLOTS, pixels), jnp.bfloat16),
        ],
        compiler_params=pltpu.CompilerParams(vmem_limit_bytes=50 * 2**20),
        name="front",
    )(pair, bins, core, images, col_table, row_table, ctf_table, slots_row, weight_cols)


def score_kernel(w_ref, p_ref, best_ref, acc):
    step = pl.program_id(0)

    @pl.when(step == 0)
    def _():
        acc[...] = jnp.zeros_like(acc)

    total = acc[...]
    classes, depth, orients, pixels = p_ref.shape
    for j in range(depth):
        panel = jnp.concatenate([p_ref[c, j] for c in range(classes)], axis=0)
        total = total + lax.dot_general(
            panel, w_ref[j], (((1,), (1,)), ((), ())), preferred_element_type=jnp.float32
        )
    acc[...] = total

    @pl.when(step == pl.num_programs(0) - 1)
    def _():
        scale = 1.0 / math.sqrt(pl.num_programs(0) * depth * pixels)
        best_ref[...] = jnp.max(total * scale, axis=0, keepdims=True)


def score(w2, panel, depth=16):
    rows, number, pixels = w2.shape
    classes, orients = panel.shape[0], panel.shape[2]
    return pl.pallas_call(
        score_kernel,
        grid=(rows // depth,),
        in_specs=[
            pl.BlockSpec((depth, number, pixels), lambda i: (i, 0, 0)),
            pl.BlockSpec((classes, depth, orients, pixels), lambda i: (0, i, 0, 0)),
        ],
        out_specs=pl.BlockSpec((1, number), lambda i: (0, 0)),
        scratch_shapes=[pltpu.VMEM((classes * orients, number), jnp.float32)],
        out_shape=jax.ShapeDtypeStruct((1, number), jnp.float32),
        compiler_params=pltpu.CompilerParams(vmem_limit_bytes=32 * 2**20),
        name="score",
    )(w2, panel)


def power_kernel(tally_ref, ctf_ref, slot_ref, wt_ref, start_ref, out_ref, squares, scr):
    bin_count, rows, pixels = ctf_ref.shape
    orients = wt_ref.shape[1]
    for b in range(bin_count):
        squares[b] = ctf_ref[b] * ctf_ref[b]
    for o in range(orients):
        value = squares[0] * tally_ref[o * bin_count]
        for b in range(1, bin_count):
            value = value + squares[b] * tally_ref[o * bin_count + b]
        value = value * wt_ref[:, o : o + 1]
        for part in range(3):
            piece = value.astype(jnp.bfloat16)
            scr[pl.ds(o * rows, rows), pl.ds(part * pixels, pixels)] = piece
            value = value - piece.astype(jnp.float32)
    target = lax.broadcasted_iota(jnp.int32, (out_ref.shape[0], orients * rows), 0) + start_ref[0]
    hot = jnp.where(target == slot_ref[...], 1.0, 0.0).astype(jnp.bfloat16)
    slab = jnp.dot(hot, scr[...], preferred_element_type=jnp.float32)
    out_ref[...] = (
        slab[:, 2 * pixels :] + slab[:, pixels : 2 * pixels]
    ) + slab[:, :pixels]


def power_slab(own_tally, ctf_table, slots_row, weight_cols, start, slab_rows):
    bin_count, rows, pixels = ctf_table.shape
    orients = weight_cols.shape[1]
    vmem = pl.BlockSpec(memory_space=pltpu.VMEM)
    smem = pl.BlockSpec(memory_space=pltpu.SMEM)
    return pl.pallas_call(
        power_kernel,
        in_specs=[smem, vmem, vmem, vmem, smem],
        out_specs=vmem,
        out_shape=jax.ShapeDtypeStruct((slab_rows, pixels), jnp.float32),
        scratch_shapes=[
            pltpu.VMEM((bin_count, rows, pixels), jnp.float32),
            pltpu.VMEM((orients * rows, 3 * pixels), jnp.bfloat16),
        ],
        compiler_params=pltpu.CompilerParams(vmem_limit_bytes=16 * 2**20),
        name="power",
    )(own_tally, ctf_table, slots_row, weight_cols, start)


def swap(value, axis, mask):
    size = lax.axis_size(axis)
    return lax.ppermute(value, axis, [(i, i ^ mask) for i in range(size)])


def on_device(
    images, ctf_table, defocus_bin, projections, best_class, best_orient, slice_slots, slot_weight
):
    orients = projections.shape[1]
    bin_count = ctf_table.shape[0]
    classes, imgs = lax.axis_size("cls"), lax.axis_size("img")
    my_cls, my_img = lax.axis_index("cls"), lax.axis_index("img")
    core, my_z = my_cls % 2, my_cls // 2
    groups, slab_rows = classes // 2, SLOTS // imgs
    pixels = images.shape[1]

    panel = lax.all_gather(jnp.transpose(projections, (0, 2, 1, 3)), "cls", axis=0, tiled=True)

    class_ids = best_class[:, 0]
    pair = class_ids * orients + best_orient
    tally_key = pair * bin_count + defocus_bin
    tally_hot = tally_key[:, None] == jnp.arange(classes * orients * bin_count, dtype=jnp.int32)
    tallies = lax.psum(jnp.sum(tally_hot.astype(jnp.float32), axis=0), ("img", "cls"))
    own_tally = lax.dynamic_slice_in_dim(
        tallies, my_cls * (orients * bin_count), orients * bin_count
    )

    slots_row = slice_slots.reshape(1, -1)
    weight_cols = slot_weight.T
    w2, keep, send = front(
        images, ctf_table, pair, defocus_bin, core[None], slots_row, weight_cols, classes
    )
    best = score(w2, panel)
    weight_slab = power_slab(
        own_tally, ctf_table, slots_row, weight_cols, (my_img * slab_rows)[None], slab_rows
    )

    chip = keep + swap(send, "cls", 1).astype(jnp.float32)
    chip = chip.reshape(groups, imgs, slab_rows, pixels)
    part = lambda mask: lax.dynamic_index_in_dim(chip, my_img ^ mask, 1, keepdims=False)
    own = part(0)
    for got in [swap(part(m).astype(jnp.bfloat16), "img", m) for m in range(1, imgs)]:
        own = own + got.astype(jnp.float32)
    part_z = lambda mask: lax.dynamic_index_in_dim(own, my_z ^ mask, 0, keepdims=False)
    data = part_z(0)
    for got in [swap(part_z(m).astype(jnp.bfloat16), "cls", 2 * m) for m in range(1, groups)]:
        data = data + got.astype(jnp.float32)
    return (best.reshape(-1), data[None], weight_slab[None])


def solution(mesh):
    return jax.shard_map(
        on_device,
        mesh=mesh,
        in_specs=(
            P(("img", "cls"), None, None),
            P(),
            P(("img", "cls")),
            P("cls", None, None, None),
            P(("img", "cls"), None),
            P(("img", "cls")),
            P(),
            P(),
        ),
        out_specs=(P(("img", "cls")), P("cls", "img", None), P("cls", "img", None)),
        check_vma=False,
    )
```

```python
import functools
import math

import jax
import jax.numpy as jnp
import numpy as np
from jax import lax
from jax.experimental import pallas as pl
from jax.experimental.pallas import tpu as pltpu
from jax.sharding import PartitionSpec as P

SLOTS = 512
BLOCK = 16


def dft_tables(pixels):
    half = pixels // 2
    position = np.arange(pixels)
    norm = 1.0 / math.sqrt(pixels)
    angle_cols = (position[:, None] * np.arange(half)[None, :] % pixels) * (2.0 * math.pi / pixels)
    col_table = np.concatenate([np.cos(angle_cols), -np.sin(angle_cols)], axis=1) * norm
    angle_rows = ((np.arange(half) - half // 2)[:, None] * position[None, :] % pixels) * (
        2.0 * math.pi / pixels
    )
    row_table = np.concatenate([np.cos(angle_rows), np.sin(angle_rows)], axis=0) * norm
    return jnp.asarray(np.stack([col_table, row_table]).astype(np.float32), jnp.bfloat16)


def front_kernel(
    blocks, class_ref, orient_ref, bin_ref, img_ref, table_ref, ctf_ref, slot_ref, wt_ref, w2_ref,
    keep_ref, send_ref, count_ref, acc, wscr, hot, value_scr, counts, wt_scr,
):
    step = pl.program_id(0)
    half = table_ref.shape[1] // 2
    orients, rows = wt_ref.shape
    number = img_ref.shape[0]

    @pl.when(step == 0)
    def _():
        acc[...] = jnp.zeros_like(acc)
        counts[...] = jnp.zeros_like(counts)
        wt_scr[...] = jnp.transpose(wt_ref[...])
        slots = lax.broadcasted_iota(jnp.int32, (hot.shape[0], rows), 0)
        for o in range(orients):
            hot[:, pl.ds(o * rows, rows)] = jnp.where(
                slots == slot_ref[o : o + 1, :], 1.0, 0.0
            ).astype(jnp.bfloat16)

    @pl.when(step < blocks)
    def _():
        lane = lax.broadcasted_iota(jnp.int32, (1, counts.shape[2]), 1)
        for i in range(number):
            one = jnp.dot(img_ref[i], table_ref[0], preferred_element_type=jnp.float32)
            both = jnp.dot(
                table_ref[1], one.astype(jnp.bfloat16), preferred_element_type=jnp.float32
            )
            index = step * number + i
            which_bin = bin_ref[index]
            which_class, which_orient = class_ref[index], orient_ref[index]
            which_pair = which_class * orients + which_orient
            counted = (which_class, pl.ds(which_orient, 1), slice(None))
            counts[counted] += jnp.where(lane == which_bin, 1.0, 0.0)
            real = both[:rows, :half] + both[rows:, half:]
            imag = both[:rows, half:] - both[rows:, :half]
            for part, spec in enumerate((real, imag)):
                lanes = pl.ds(part * half, half)
                weighted = (spec * ctf_ref[which_bin, :, lanes]).astype(jnp.bfloat16)
                weighted = weighted.astype(jnp.float32)
                acc[which_pair, :, lanes] += weighted
                wscr[part, pl.ds(i * (rows + 8), rows), :] = weighted
        for j in range(rows):
            w2_ref[j] = jnp.concatenate(
                [
                    wscr[part, pl.ds(j, number, stride=rows + 8), :]
                    for part in range(2)
                ],
                axis=1,
            ).astype(jnp.bfloat16)

    @pl.when(step >= blocks)
    def _():
        z = step - blocks
        core = lax.axis_index("cls") % 2
        for part, which in enumerate((2 * z + core, 2 * z + 1 - core)):
            for o in range(orients):
                value = acc[which * orients + o] * wt_scr[:, o : o + 1]
                value_scr[pl.ds(o * rows, rows), pl.ds(part * 2 * half, 2 * half)] = value.astype(
                    jnp.bfloat16
                )
        slab = jnp.dot(hot[...], value_scr[...], preferred_element_type=jnp.float32)
        keep_ref[0] = slab[:, : 2 * half]
        send_ref[0, : SLOTS] = slab[:, 2 * half :].astype(jnp.bfloat16)
        send_ref[0, SLOTS :, : half] = counts[2 * z + 1 - core].astype(jnp.bfloat16)
        send_ref[0, SLOTS :, half :] = jnp.zeros((orients, half), jnp.bfloat16)
        count_ref[0] = counts[2 * z + core]


def front(images, ctf_table, class_ids, orient_ids, bins, slice_slots, slot_weight, classes):
    number, pixels = images.shape[0], images.shape[1]
    bin_count, rows = ctf_table.shape[0], ctf_table.shape[1]
    orients = slot_weight.shape[0]
    blocks, groups = number // BLOCK, classes // 2
    at_block = lambda i: jnp.minimum(i, blocks - 1)
    at_group = lambda i: jnp.maximum(i - blocks, 0)
    whole = lambda shape: pl.BlockSpec(
        shape, lambda i, *_: (0,) * len(shape), pipeline_mode=pl.Buffered(1)
    )
    return pl.pallas_call(
        functools.partial(front_kernel, blocks),
        grid_spec=pltpu.PrefetchScalarGridSpec(
            num_scalar_prefetch=3,
            grid=(blocks + groups,),
            in_specs=[
                pl.BlockSpec((BLOCK, pixels, pixels), lambda i, *_: (at_block(i), 0, 0)),
                whole((2, pixels, pixels)),
                whole((bin_count, rows, pixels)),
                whole((orients, rows)),
                whole((orients, rows)),
            ],
            out_specs=[
                pl.BlockSpec((rows, BLOCK, pixels), lambda i, *_: (0, at_block(i), 0)),
                pl.BlockSpec((1, SLOTS, pixels), lambda i, *_: (at_group(i), 0, 0)),
                pl.BlockSpec((1, SLOTS + orients, pixels), lambda i, *_: (at_group(i), 0, 0)),
                pl.BlockSpec((1, orients, pixels // 2), lambda i, *_: (at_group(i), 0, 0)),
            ],
            scratch_shapes=[
                pltpu.VMEM((classes * orients, rows, pixels), jnp.float32),
                pltpu.VMEM((2, BLOCK * (rows + 8), pixels // 2), jnp.float32),
                pltpu.VMEM((SLOTS, orients * rows), jnp.bfloat16),
                pltpu.VMEM((orients * rows, 2 * pixels), jnp.bfloat16),
                pltpu.VMEM((classes, orients, pixels // 2), jnp.float32),
                pltpu.VMEM((rows, orients), jnp.float32),
            ],
        ),
        out_shape=[
            jax.ShapeDtypeStruct((rows, number, pixels), jnp.bfloat16),
            jax.ShapeDtypeStruct((groups, SLOTS, pixels), jnp.float32),
            jax.ShapeDtypeStruct((groups, SLOTS + orients, pixels), jnp.bfloat16),
            jax.ShapeDtypeStruct((groups, orients, pixels // 2), jnp.float32),
        ],
        compiler_params=pltpu.CompilerParams(vmem_limit_bytes=60 * 2**20),
        cost_estimate=pl.CostEstimate(
            flops=8 * number * pixels**3, bytes_accessed=number * pixels**2 * 4, transcendentals=0
        ),
        name="front",
    )(class_ids, orient_ids, bins, images, dft_tables(pixels), ctf_table, slice_slots, slot_weight)


def score_kernel(w_ref, panel_ref, best_ref, acc):
    step = pl.program_id(0)

    @pl.when(step == 0)
    def _():
        acc[...] = jnp.zeros_like(acc)

    total = acc[...]
    for j in range(w_ref.shape[0]):
        panel = [panel_ref[c, j] for c in range(panel_ref.shape[0])]
        total = total + lax.dot_general(
            jnp.concatenate(panel, axis=0),
            w_ref[j],
            (((1,), (1,)), ((), ())),
            preferred_element_type=jnp.float32,
        )
    acc[...] = total

    @pl.when(step == pl.num_programs(0) - 1)
    def _():
        scale = 1.0 / math.sqrt(pl.num_programs(0) * w_ref.shape[0] * w_ref.shape[2])
        best_ref[...] = jnp.max(acc[...] * scale, axis=0, keepdims=True)


def score(w2, panel, depth=16):
    rows, number, pixels = w2.shape
    classes, orients = panel.shape[0], panel.shape[2]
    return pl.pallas_call(
        score_kernel,
        grid=(rows // depth,),
        in_specs=[
            pl.BlockSpec((depth, number, pixels), lambda i: (i, 0, 0)),
            pl.BlockSpec((classes, depth, orients, pixels), lambda i: (0, i, 0, 0)),
        ],
        out_specs=pl.BlockSpec((1, number), lambda i: (0, 0)),
        scratch_shapes=[pltpu.VMEM((classes * orients, number), jnp.float32)],
        out_shape=jax.ShapeDtypeStruct((1, number), jnp.float32),
        compiler_params=pltpu.CompilerParams(vmem_limit_bytes=60 * 2**20),
        name="score",
    )(w2, panel)


def chip_kernel(masks, keep_ref, count_ref, got_ref, own_ref, own_count_ref, *outs):
    size = own_ref.shape[1]
    slots = keep_ref.shape[1]
    lanes = count_ref.shape[2]
    count = count_ref[...] + got_ref[:, pl.ds(slots, 8), pl.ds(0, lanes)].astype(jnp.float32)
    own_count_ref[...] = count

    def part(mask):
        rows = pl.ds(pl.multiple_of((lax.axis_index("img") ^ mask) * size, size), size)
        return keep_ref[:, rows, :] + got_ref[:, rows, :].astype(jnp.float32)

    own_ref[...] = part(0)
    for mask, out_ref in zip(masks, outs, strict=True):
        out_ref[:, pl.ds(0, size), :] = part(mask).astype(jnp.bfloat16)
        tail = count.astype(jnp.bfloat16)
        out_ref[:, pl.ds(size, 8), :] = jnp.concatenate([tail, jnp.zeros_like(tail)], axis=2)


def chip_sum(keep, count, got, imgs):
    groups, slots, pixels = keep.shape
    size = slots // imgs
    masks = tuple(range(1, imgs))
    at = lambda shape: pl.BlockSpec((1, *shape[1:]), lambda i: (i, 0, 0))
    out_shape = [
        jax.ShapeDtypeStruct((groups, size, pixels), jnp.float32),
        jax.ShapeDtypeStruct(count.shape, jnp.float32),
    ] + [jax.ShapeDtypeStruct((groups, size + 8, pixels), jnp.bfloat16)] * (imgs - 1)
    return pl.pallas_call(
        functools.partial(chip_kernel, masks),
        grid=(groups,),
        in_specs=[at(keep.shape), at(count.shape), at(got.shape)],
        out_specs=[at(out.shape) for out in out_shape],
        out_shape=out_shape,
        compiler_params=pltpu.CompilerParams(vmem_limit_bytes=12 * 2**20),
        name="chip_sum",
    )(keep, count, got)


def plane_kernel(masks, own_ref, count_ref, *refs):
    gots, outs = refs[: len(refs) - len(masks) - 2], refs[len(refs) - len(masks) - 2 :]
    data_ref, data_count_ref, sends = outs[0], outs[1], outs[2:]
    size, lanes = own_ref.shape[1], count_ref.shape[2]

    def part(mask):
        z = (lax.axis_index("cls") // 2) ^ mask
        data, count = own_ref[z], count_ref[z]
        for got in gots:
            data = data + got[z, pl.ds(0, size), :].astype(jnp.float32)
            count = count + got[z, pl.ds(size, 8), pl.ds(0, lanes)].astype(jnp.float32)
        return data, count

    data_ref[...], data_count_ref[...] = part(0)
    for mask, send_ref in zip(masks, sends, strict=True):
        data, count = part(mask)
        high = jnp.floor(count * (1.0 / 128.0)) * 128.0
        send_ref[pl.ds(0, size), :] = data.astype(jnp.bfloat16)
        send_ref[pl.ds(size, 8), :] = jnp.concatenate([high, count - high], axis=1).astype(
            jnp.bfloat16
        )


def plane_sum(own, count, gots):
    groups, size, pixels = own.shape
    vmem = pl.BlockSpec()
    masks = tuple(range(1, groups))
    return pl.pallas_call(
        functools.partial(plane_kernel, masks),
        in_specs=[vmem] * (2 + len(gots)),
        out_specs=[vmem] * (groups + 1),
        out_shape=[
            jax.ShapeDtypeStruct((size, pixels), jnp.float32),
            jax.ShapeDtypeStruct(count.shape[1:], jnp.float32),
        ]
        + [jax.ShapeDtypeStruct((size + 8, pixels), jnp.bfloat16)] * (groups - 1),
        compiler_params=pltpu.CompilerParams(vmem_limit_bytes=12 * 2**20),
        name="plane_sum",
    )(own, count, *gots)


def final_kernel(ctf_ref, slot_ref, wt_ref, own_ref, count_ref, *refs):
    gots, (data_ref, weight_ref, squares, scr) = refs[:-4], refs[-4:]
    bin_count, rows, pixels = ctf_ref.shape
    size, orients, lanes = own_ref.shape[0], wt_ref.shape[0], count_ref.shape[1]
    wt_cols = jnp.transpose(wt_ref[...])
    data, count = own_ref[...], count_ref[...]
    for got in gots:
        data = data + got[pl.ds(0, size), :].astype(jnp.float32)
        tail = got[pl.ds(size, 8), :].astype(jnp.float32)
        count = count + (tail[:, :lanes] + tail[:, lanes:])
    data_ref[...] = data
    for b in range(bin_count):
        squares[b] = ctf_ref[b] * ctf_ref[b]
    for o in range(orients):
        value = squares[0] * count[o : o + 1, 0:1]
        for b in range(1, bin_count):
            value = value + squares[b] * count[o : o + 1, b : b + 1]
        value = value * wt_cols[:, o : o + 1]
        for part in range(3):
            piece = value.astype(jnp.bfloat16)
            scr[pl.ds(o * rows, rows), pl.ds(part * pixels, pixels)] = piece
            value = value - piece.astype(jnp.float32)
    target = lax.broadcasted_iota(jnp.int32, (size, rows), 0) + lax.axis_index("img") * size
    hot = jnp.concatenate(
        [
            jnp.where(target == slot_ref[o : o + 1, :], 1.0, 0.0).astype(jnp.bfloat16)
            for o in range(orients)
        ],
        axis=1,
    )
    slab = jnp.dot(hot, scr[...], preferred_element_type=jnp.float32)
    weight_ref[...] = (slab[:, 2 * pixels :] + slab[:, pixels : 2 * pixels]) + slab[:, :pixels]


def final_sum(ctf_table, slice_slots, slot_weight, own, count, gots):
    bin_count, rows, pixels = ctf_table.shape
    orients = slot_weight.shape[0]
    vmem = pl.BlockSpec()
    return pl.pallas_call(
        final_kernel,
        in_specs=[vmem] * (5 + len(gots)),
        out_specs=[vmem, vmem],
        out_shape=[jax.ShapeDtypeStruct(own.shape, jnp.float32)] * 2,
        scratch_shapes=[
            pltpu.VMEM((bin_count, rows, pixels), jnp.float32),
            pltpu.VMEM((orients * rows, 3 * pixels), jnp.bfloat16),
        ],
        compiler_params=pltpu.CompilerParams(vmem_limit_bytes=12 * 2**20),
        name="final_sum",
    )(ctf_table, slice_slots, slot_weight, own, count, *gots)


def swap(value, axis, mask):
    size = lax.axis_size(axis)
    return lax.ppermute(value, axis, [(i, i ^ mask) for i in range(size)])


def on_device(
    images, ctf_table, defocus_bin, projections, best_class, best_orient, slice_slots, slot_weight
):
    classes, imgs = lax.axis_size("cls"), lax.axis_size("img")
    own_panel = jnp.transpose(projections, (0, 2, 1, 3))
    panel = lax.all_gather(own_panel, "cls", axis=0, tiled=True)
    w2, keep, send, count = front(
        images,
        ctf_table,
        best_class.reshape(-1),
        best_orient,
        defocus_bin,
        slice_slots,
        slot_weight,
        classes,
    )
    got = swap(send, "cls", 1)
    own, own_count, *parts = chip_sum(keep, count, got, imgs)
    gots = [swap(part, "img", m + 1) for m, part in enumerate(parts)]
    data, data_count, *parts = plane_sum(own, own_count, gots)
    gots = [swap(part, "cls", 2 * (m + 1)) for m, part in enumerate(parts)]
    best = score(w2, panel)
    gots, best = lax.optimization_barrier((gots, best))
    data, weight = final_sum(ctf_table, slice_slots, slot_weight, data, data_count, gots)
    return (best.reshape(-1), data[None], weight[None])


def solution(mesh):
    return jax.shard_map(
        on_device,
        mesh=mesh,
        in_specs=(
            P(("img", "cls"), None, None),
            P(),
            P(("img", "cls")),
            P("cls", None, None, None),
            P(("img", "cls"), None),
            P(("img", "cls")),
            P(),
            P(),
        ),
        out_specs=(P(("img", "cls")), P("cls", "img", None), P("cls", "img", None)),
        check_vma=False,
    )
```

```python
import functools
import math

import jax
import jax.numpy as jnp
import numpy as np
from jax import lax
from jax.experimental import pallas as pl
from jax.experimental.pallas import tpu as pltpu
from jax.sharding import PartitionSpec as P

SLOTS = 512
BLOCK = 16


def dft_tables(pixels):
    half = pixels // 2
    position = np.arange(pixels)
    norm = 1.0 / math.sqrt(pixels)
    angle_cols = (position[:, None] * np.arange(half)[None, :] % pixels) * (2.0 * math.pi / pixels)
    col_table = np.concatenate([np.cos(angle_cols), -np.sin(angle_cols)], axis=1) * norm
    angle_rows = ((np.arange(half) - half // 2)[:, None] * position[None, :] % pixels) * (
        2.0 * math.pi / pixels
    )
    row_table = np.concatenate([np.cos(angle_rows), np.sin(angle_rows)], axis=0) * norm
    return jnp.asarray(np.stack([col_table, row_table]).astype(np.float32), jnp.bfloat16)


def front_kernel(
    blocks, class_ref, orient_ref, bin_ref, img_ref, table_ref, ctf_ref, slot_ref, wt_ref, w2_ref,
    keep_ref, send_ref, count_ref, acc, wscr, hot, value_scr, counts, wt_scr,
):
    step = pl.program_id(0)
    half = table_ref.shape[1] // 2
    orients, rows = wt_ref.shape
    number = img_ref.shape[0]

    @pl.when(step == 0)
    def _():
        acc[...] = jnp.zeros_like(acc)
        counts[...] = jnp.zeros_like(counts)
        wt_scr[...] = jnp.transpose(wt_ref[...])
        slots = lax.broadcasted_iota(jnp.int32, (hot.shape[0], rows), 0)
        for o in range(orients):
            hot[:, pl.ds(o * rows, rows)] = jnp.where(
                slots == slot_ref[o : o + 1, :], 1.0, 0.0
            ).astype(jnp.bfloat16)

    @pl.when(step < blocks)
    def _():
        lane = lax.broadcasted_iota(jnp.int32, (1, counts.shape[2]), 1)
        for i in range(number):
            one = jnp.dot(img_ref[i], table_ref[0], preferred_element_type=jnp.float32)
            both = jnp.dot(
                table_ref[1], one.astype(jnp.bfloat16), preferred_element_type=jnp.float32
            )
            index = step * number + i
            which_bin = bin_ref[index]
            which_class, which_orient = class_ref[index], orient_ref[index]
            which_pair = which_class * orients + which_orient
            counted = (which_class, pl.ds(which_orient, 1), slice(None))
            counts[counted] += jnp.where(lane == which_bin, 1.0, 0.0)
            real = both[:rows, :half] + both[rows:, half:]
            imag = both[:rows, half:] - both[rows:, :half]
            for part, spec in enumerate((real, imag)):
                lanes = pl.ds(part * half, half)
                weighted = (spec * ctf_ref[which_bin, :, lanes]).astype(jnp.bfloat16)
                weighted = weighted.astype(jnp.float32)
                acc[which_pair, :, lanes] += weighted
                wscr[part, pl.ds(i * (rows + 8), rows), :] = weighted
        for j in range(rows):
            w2_ref[j] = jnp.concatenate(
                [
                    wscr[part, pl.ds(j, number, stride=rows + 8), :]
                    for part in range(2)
                ],
                axis=1,
            ).astype(jnp.bfloat16)

    @pl.when(step >= blocks)
    def _():
        z = step - blocks
        core = lax.axis_index("cls") % 2
        for part, which in enumerate((2 * z + core, 2 * z + 1 - core)):
            for o in range(orients):
                value = acc[which * orients + o] * wt_scr[:, o : o + 1]
                value_scr[pl.ds(o * rows, rows), pl.ds(part * 2 * half, 2 * half)] = value.astype(
                    jnp.bfloat16
                )
        slab = jnp.dot(hot[...], value_scr[...], preferred_element_type=jnp.float32)
        keep_ref[0] = slab[:, : 2 * half]
        send_ref[0, : SLOTS] = slab[:, 2 * half :].astype(jnp.bfloat16)
        send_ref[0, SLOTS :, : half] = counts[2 * z + 1 - core].astype(jnp.bfloat16)
        send_ref[0, SLOTS :, half :] = jnp.zeros((orients, half), jnp.bfloat16)
        count_ref[0] = counts[2 * z + core]


def front(images, ctf_table, class_ids, orient_ids, bins, slice_slots, slot_weight, classes):
    number, pixels = images.shape[0], images.shape[1]
    bin_count, rows = ctf_table.shape[0], ctf_table.shape[1]
    orients = slot_weight.shape[0]
    blocks, groups = number // BLOCK, classes // 2
    at_block = lambda i: jnp.minimum(i, blocks - 1)
    at_group = lambda i: jnp.maximum(i - blocks, 0)
    whole = lambda shape: pl.BlockSpec(
        shape, lambda i, *_: (0,) * len(shape), pipeline_mode=pl.Buffered(1)
    )
    return pl.pallas_call(
        functools.partial(front_kernel, blocks),
        grid_spec=pltpu.PrefetchScalarGridSpec(
            num_scalar_prefetch=0,
            grid=(blocks + groups,),
            in_specs=[
                *[pl.BlockSpec((number,), lambda i: (0,), memory_space=pltpu.SMEM)] * 3,
                pl.BlockSpec((BLOCK, pixels, pixels), lambda i, *_: (at_block(i), 0, 0)),
                whole((2, pixels, pixels)),
                whole((bin_count, rows, pixels)),
                whole((orients, rows)),
                whole((orients, rows)),
            ],
            out_specs=[
                pl.BlockSpec((rows, BLOCK, pixels), lambda i, *_: (0, at_block(i), 0)),
                pl.BlockSpec((1, SLOTS, pixels), lambda i, *_: (at_group(i), 0, 0)),
                pl.BlockSpec((1, SLOTS + orients, pixels), lambda i, *_: (at_group(i), 0, 0)),
                pl.BlockSpec((1, orients, pixels // 2), lambda i, *_: (at_group(i), 0, 0)),
            ],
            scratch_shapes=[
                pltpu.VMEM((classes * orients, rows, pixels), jnp.float32),
                pltpu.VMEM((2, BLOCK * (rows + 8), pixels // 2), jnp.float32),
                pltpu.VMEM((SLOTS, orients * rows), jnp.bfloat16),
                pltpu.VMEM((orients * rows, 2 * pixels), jnp.bfloat16),
                pltpu.VMEM((classes, orients, pixels // 2), jnp.float32),
                pltpu.VMEM((rows, orients), jnp.float32),
            ],
        ),
        out_shape=[
            pltpu.HBM((rows, number, pixels), jnp.bfloat16),
            jax.ShapeDtypeStruct((groups, SLOTS, pixels), jnp.float32),
            jax.ShapeDtypeStruct((groups, SLOTS + orients, pixels), jnp.bfloat16),
            jax.ShapeDtypeStruct((groups, orients, pixels // 2), jnp.float32),
        ],
        compiler_params=pltpu.CompilerParams(vmem_limit_bytes=40 * 2**20),
        cost_estimate=pl.CostEstimate(
            flops=8 * number * pixels**3, bytes_accessed=number * pixels**2 * 4, transcendentals=0
        ),
        name="front",
    )(
        *(
            pltpu.with_memory_space_constraint(x, pltpu.HBM)
            for x in (
                class_ids, orient_ids, bins, images, dft_tables(pixels), ctf_table, slice_slots, slot_weight,
            )
        )
    )


def score_kernel(orients, last, sum_ref, w_ref, *refs):
    panels, (out_ref, even, odd) = refs[:-3], refs[-3:]
    step = pl.program_id(0)
    number, pixels = w_ref.shape[1], w_ref.shape[2]

    @pl.when(step == 0)
    def _():
        even[...] = sum_ref[0]
        odd[...] = sum_ref[1]

    if len(panels) == 2:
        blocks = [(ref, c) for ref in panels for c in range(ref.shape[0])]
    else:
        z, core = lax.axis_index("cls") // 2, lax.axis_index("cls") % 2
        groups = range(panels[0].shape[0] // 2)
        blocks = [(panels[0], 2 * (z ^ m) + c) for c in (core, 1 - core) for m in groups]
    totals = [even[...], odd[...]]
    for pair in range(w_ref.shape[0] // 2):
        rows = pl.ds(pair * 2 * orients, 2 * orients)
        both = jnp.concatenate([ref[c, rows, :] for ref, c in blocks], axis=0)
        images = w_ref[2 * pair : 2 * pair + 2].reshape(2 * number, pixels)
        scores = lax.dot_general(
            images, both, (((1,), (1,)), ((), ())), preferred_element_type=jnp.float32
        )
        totals = [totals[0] + scores[:number], totals[1] + scores[number:]]
    even[...], odd[...] = totals

    @pl.when(step == pl.num_programs(0) - 1)
    def _():
        if last is None:
            out_ref[0] = even[...]
            out_ref[1] = odd[...]
        else:
            halves = (-1, 2, orients, number)
            sums = jnp.transpose(even[...]).reshape(halves)[:, 0]
            sums = (sums + jnp.transpose(odd[...]).reshape(halves)[:, 1]) * last
            out_ref[...] = jnp.max(jnp.max(sums, axis=0), axis=0, keepdims=True)


def score(w2, panels, sums, first, last=None, depth=32):
    number, pixels = w2.shape[1], w2.shape[2]
    orients = 8
    steps = panels[0].shape[1] // (depth * orients)
    hbm = lambda x: pltpu.with_memory_space_constraint(x, pltpu.HBM)
    whole = lambda shape: pl.BlockSpec(shape, lambda i: (0,) * len(shape))
    out_shape = sums.shape if last is None else (1, number)
    return pl.pallas_call(
        functools.partial(score_kernel, orients, last),
        grid=(steps,),
        in_specs=[whole(sums.shape)]
        + [pl.BlockSpec((depth, number, pixels), lambda i: (first // depth + i, 0, 0))]
        + [
            pl.BlockSpec((panel.shape[0], depth * orients, pixels), lambda i: (0, i, 0))
            for panel in panels
        ],
        out_specs=whole(out_shape),
        scratch_shapes=[pltpu.VMEM(sums.shape[1:], jnp.float32)] * 2,
        out_shape=jax.ShapeDtypeStruct(out_shape, jnp.float32),
        compiler_params=pltpu.CompilerParams(vmem_limit_bytes=20 * 2**20),
        name="score",
    )(sums, hbm(w2), *(hbm(panel) for panel in panels))


def chip_kernel(masks, keep_ref, count_ref, got_ref, own_ref, own_count_ref, *outs):
    size = own_ref.shape[1]
    slots = keep_ref.shape[1]
    lanes = count_ref.shape[2]
    count = count_ref[...] + got_ref[:, pl.ds(slots, 8), pl.ds(0, lanes)].astype(jnp.float32)
    own_count_ref[...] = count

    def part(mask):
        rows = pl.ds(pl.multiple_of((lax.axis_index("img") ^ mask) * size, size), size)
        return keep_ref[:, rows, :] + got_ref[:, rows, :].astype(jnp.float32)

    own_ref[...] = part(0)
    for mask, out_ref in zip(masks, outs, strict=True):
        out_ref[:, pl.ds(0, size), :] = part(mask).astype(jnp.bfloat16)
        tail = count.astype(jnp.bfloat16)
        out_ref[:, pl.ds(size, 8), :] = jnp.concatenate([tail, jnp.zeros_like(tail)], axis=2)


def chip_sum(keep, count, got, imgs):
    groups, slots, pixels = keep.shape
    size = slots // imgs
    masks = tuple(range(1, imgs))
    at = lambda shape: pl.BlockSpec((1, *shape[1:]), lambda i: (i, 0, 0))
    out_shape = [
        jax.ShapeDtypeStruct((groups, size, pixels), jnp.float32),
        jax.ShapeDtypeStruct(count.shape, jnp.float32),
    ] + [jax.ShapeDtypeStruct((groups, size + 8, pixels), jnp.bfloat16)] * (imgs - 1)
    return pl.pallas_call(
        functools.partial(chip_kernel, masks),
        grid=(groups,),
        in_specs=[at(keep.shape), at(count.shape), at(got.shape)],
        out_specs=[at(out.shape) for out in out_shape],
        out_shape=out_shape,
        compiler_params=pltpu.CompilerParams(vmem_limit_bytes=12 * 2**20),
        name="chip_sum",
    )(keep, count, got)


def plane_kernel(masks, own_ref, count_ref, *refs):
    gots, outs = refs[: len(refs) - len(masks) - 2], refs[len(refs) - len(masks) - 2 :]
    data_ref, data_count_ref, sends = outs[0], outs[1], outs[2:]
    size, lanes = own_ref.shape[1], count_ref.shape[2]

    def part(mask):
        z = (lax.axis_index("cls") // 2) ^ mask
        data, count = own_ref[z], count_ref[z]
        for got in gots:
            data = data + got[z, pl.ds(0, size), :].astype(jnp.float32)
            count = count + got[z, pl.ds(size, 8), pl.ds(0, lanes)].astype(jnp.float32)
        return data, count

    data_ref[...], data_count_ref[...] = part(0)
    for mask, send_ref in zip(masks, sends, strict=True):
        data, count = part(mask)
        high = jnp.floor(count * (1.0 / 128.0)) * 128.0
        send_ref[pl.ds(0, size), :] = data.astype(jnp.bfloat16)
        send_ref[pl.ds(size, 8), :] = jnp.concatenate([high, count - high], axis=1).astype(
            jnp.bfloat16
        )


def plane_sum(own, count, gots):
    groups, size, pixels = own.shape
    vmem = pl.BlockSpec()
    masks = tuple(range(1, groups))
    return pl.pallas_call(
        functools.partial(plane_kernel, masks),
        in_specs=[vmem] * (2 + len(gots)),
        out_specs=[vmem] * (groups + 1),
        out_shape=[
            jax.ShapeDtypeStruct((size, pixels), jnp.float32),
            jax.ShapeDtypeStruct(count.shape[1:], jnp.float32),
        ]
        + [jax.ShapeDtypeStruct((size + 8, pixels), jnp.bfloat16)] * (groups - 1),
        compiler_params=pltpu.CompilerParams(vmem_limit_bytes=12 * 2**20),
        name="plane_sum",
    )(own, count, *gots)


def final_kernel(ctf_ref, slot_ref, wt_ref, own_ref, count_ref, *refs):
    gots, (data_ref, weight_ref, squares, scr) = refs[:-4], refs[-4:]
    bin_count, rows, pixels = ctf_ref.shape
    size, orients, lanes = own_ref.shape[0], wt_ref.shape[0], count_ref.shape[1]
    wt_cols = jnp.transpose(wt_ref[...])
    data, count = own_ref[...], count_ref[...]
    for got in gots:
        data = data + got[pl.ds(0, size), :].astype(jnp.float32)
        tail = got[pl.ds(size, 8), :].astype(jnp.float32)
        count = count + (tail[:, :lanes] + tail[:, lanes:])
    data_ref[...] = data
    for b in range(bin_count):
        squares[b] = ctf_ref[b] * ctf_ref[b]
    for o in range(orients):
        value = squares[0] * count[o : o + 1, 0:1]
        for b in range(1, bin_count):
            value = value + squares[b] * count[o : o + 1, b : b + 1]
        value = value * wt_cols[:, o : o + 1]
        for part in range(3):
            piece = value.astype(jnp.bfloat16)
            scr[pl.ds(o * rows, rows), pl.ds(part * pixels, pixels)] = piece
            value = value - piece.astype(jnp.float32)
    target = lax.broadcasted_iota(jnp.int32, (size, rows), 0) + lax.axis_index("img") * size
    hot = jnp.concatenate(
        [
            jnp.where(target == slot_ref[o : o + 1, :], 1.0, 0.0).astype(jnp.bfloat16)
            for o in range(orients)
        ],
        axis=1,
    )
    slab = jnp.dot(hot, scr[...], preferred_element_type=jnp.float32)
    weight_ref[...] = (slab[:, 2 * pixels :] + slab[:, pixels : 2 * pixels]) + slab[:, :pixels]


def final_sum(ctf_table, slice_slots, slot_weight, own, count, gots):
    bin_count, rows, pixels = ctf_table.shape
    orients = slot_weight.shape[0]
    vmem = pl.BlockSpec()
    return pl.pallas_call(
        final_kernel,
        in_specs=[vmem] * (5 + len(gots)),
        out_specs=[vmem, vmem],
        out_shape=[jax.ShapeDtypeStruct(own.shape, jnp.float32)] * 2,
        scratch_shapes=[
            pltpu.VMEM((bin_count, rows, pixels), jnp.float32),
            pltpu.VMEM((orients * rows, 3 * pixels), jnp.bfloat16),
        ],
        compiler_params=pltpu.CompilerParams(vmem_limit_bytes=12 * 2**20),
        name="final_sum",
    )(ctf_table, slice_slots, slot_weight, own, count, *gots)


def swap(value, axis, mask):
    size = lax.axis_size(axis)
    return lax.ppermute(value, axis, [(i, i ^ mask) for i in range(size)])


def on_device(
    images, ctf_table, defocus_bin, projections, best_class, best_orient, slice_slots, slot_weight
):
    classes, imgs = lax.axis_size("cls"), lax.axis_size("img")
    groups = classes // 2
    rows, pixels = ctf_table.shape[1], images.shape[2]
    orients = slot_weight.shape[0]
    near_rows = rows * 1 // 2
    own_panel = jnp.transpose(projections, (0, 2, 1, 3)).reshape(1, -1, pixels)
    near = own_panel[:, : near_rows * orients]
    near = [near] + [swap(near, "cls", 2 * m) for m in range(1, groups)]
    w2, keep, send, count = front(
        images,
        ctf_table,
        best_class.reshape(-1),
        best_orient,
        defocus_bin,
        slice_slots,
        slot_weight,
        classes,
    )
    send, near = lax.optimization_barrier((send, near))
    got = swap(send, "cls", 1)
    own, own_count, *parts = chip_sum(keep, count, got, imgs)
    gots = [swap(part, "img", m + 1) for m, part in enumerate(parts)]
    far = own_panel[:, near_rows * orients :]
    far = [far] + [swap(far, "cls", 2 * m) for m in range(1, groups)]
    near = jnp.concatenate(near, axis=0)
    other = swap(near, "cls", 1)
    sums = jnp.zeros((2, images.shape[0], 2 * classes * orients), jnp.float32)
    sums = score(w2, [near, other], sums, 0)
    gots, sums = lax.optimization_barrier((gots, sums))
    data, data_count, *parts = plane_sum(own, own_count, gots)
    gots = [swap(part, "cls", 2 * (m + 1)) for m, part in enumerate(parts)]
    _, far = lax.optimization_barrier((data, far))
    far = jnp.concatenate(far, axis=0)
    best = score(w2, [far, swap(far, "cls", 1)], sums, near_rows, 1.0 / math.sqrt(rows * pixels))
    gots, best = lax.optimization_barrier((gots, best))
    data, weight = final_sum(ctf_table, slice_slots, slot_weight, data, data_count, gots)
    return (best.reshape(-1), data[None], weight[None])


def solution(mesh):
    return jax.shard_map(
        on_device,
        mesh=mesh,
        in_specs=(
            P(("img", "cls"), None, None),
            P(),
            P(("img", "cls")),
            P("cls", None, None, None),
            P(("img", "cls"), None),
            P(("img", "cls")),
            P(),
            P(),
        ),
        out_specs=(P(("img", "cls")), P("cls", "img", None), P("cls", "img", None)),
        check_vma=False,
    )
```

```python
import functools
import math

import jax
import jax.numpy as jnp
import numpy as np
from jax import lax
from jax.experimental import pallas as pl
from jax.experimental.pallas import tpu as pltpu
from jax.sharding import PartitionSpec as P

SLOTS = 512
BLOCK = 16


def dft_tables(pixels):
    half = pixels // 2
    position = np.arange(pixels)
    norm = 1.0 / math.sqrt(pixels)
    angle_cols = (position[:, None] * np.arange(half)[None, :] % pixels) * (2.0 * math.pi / pixels)
    col_table = np.concatenate([np.cos(angle_cols), -np.sin(angle_cols)], axis=1) * norm
    angle_rows = ((np.arange(half) - half // 2)[:, None] * position[None, :] % pixels) * (
        2.0 * math.pi / pixels
    )
    row_table = np.concatenate([np.cos(angle_rows), np.sin(angle_rows)], axis=0) * norm
    return jnp.asarray(np.stack([col_table, row_table]).astype(np.float32), jnp.bfloat16)


def front_kernel(
    blocks, class_ref, orient_ref, bin_ref, img_ref, table_ref, ctf_ref, slot_ref, wt_ref, w2_ref,
    keep_ref, send_ref, count_ref, acc, wscr, hot, value_scr, counts, wt_scr,
):
    step = pl.program_id(0)
    half = table_ref.shape[1] // 2
    orients, rows = wt_ref.shape
    number = img_ref.shape[0]

    @pl.when(step == 0)
    def _():
        acc[...] = jnp.zeros_like(acc)
        counts[...] = jnp.zeros_like(counts)
        wt_scr[...] = jnp.transpose(wt_ref[...])
        slots = lax.broadcasted_iota(jnp.int32, (hot.shape[0], rows), 0)
        for o in range(orients):
            hot[:, pl.ds(o * rows, rows)] = jnp.where(
                slots == slot_ref[o : o + 1, :], 1.0, 0.0
            ).astype(jnp.bfloat16)

    @pl.when(step < blocks)
    def _():
        lane = lax.broadcasted_iota(jnp.int32, (1, counts.shape[2]), 1)
        for i in range(number):
            one = jnp.dot(img_ref[i], table_ref[0], preferred_element_type=jnp.float32)
            both = jnp.dot(
                table_ref[1], one.astype(jnp.bfloat16), preferred_element_type=jnp.float32
            )
            index = step * number + i
            which_bin = bin_ref[index]
            which_class, which_orient = class_ref[index], orient_ref[index]
            which_pair = which_class * orients + which_orient
            counted = (which_class, pl.ds(which_orient, 1), slice(None))
            counts[counted] += jnp.where(lane == which_bin, 1.0, 0.0)
            real = both[:rows, :half] + both[rows:, half:]
            imag = both[:rows, half:] - both[rows:, :half]
            for part, spec in enumerate((real, imag)):
                lanes = pl.ds(part * half, half)
                weighted = (spec * ctf_ref[which_bin, :, lanes]).astype(jnp.bfloat16)
                weighted = weighted.astype(jnp.float32)
                acc[which_pair, :, lanes] += weighted
                wscr[part, pl.ds(i * (rows + 8), rows), :] = weighted
        for j in range(rows):
            w2_ref[j] = jnp.concatenate(
                [
                    wscr[part, pl.ds(j, number, stride=rows + 8), :]
                    for part in range(2)
                ],
                axis=1,
            ).astype(jnp.bfloat16)

    @pl.when(step >= blocks)
    def _():
        z = step - blocks
        core = lax.axis_index("cls") % 2
        for part, which in enumerate((2 * z + core, 2 * z + 1 - core)):
            for o in range(orients):
                value = acc[which * orients + o] * wt_scr[:, o : o + 1]
                value_scr[pl.ds(o * rows, rows), pl.ds(part * 2 * half, 2 * half)] = value.astype(
                    jnp.bfloat16
                )
        slab = jnp.dot(hot[...], value_scr[...], preferred_element_type=jnp.float32)
        keep_ref[0] = slab[:, : 2 * half]
        send_ref[0, : SLOTS] = slab[:, 2 * half :].astype(jnp.bfloat16)
        send_ref[0, SLOTS :, : half] = counts[2 * z + 1 - core].astype(jnp.bfloat16)
        send_ref[0, SLOTS :, half :] = jnp.zeros((orients, half), jnp.bfloat16)
        count_ref[0] = counts[2 * z + core]


def front(images, ctf_table, class_ids, orient_ids, bins, slice_slots, slot_weight, classes):
    number, pixels = images.shape[0], images.shape[1]
    bin_count, rows = ctf_table.shape[0], ctf_table.shape[1]
    orients = slot_weight.shape[0]
    blocks, groups = number // BLOCK, classes // 2
    at_block = lambda i: jnp.minimum(i, blocks - 1)
    at_group = lambda i: jnp.maximum(i - blocks, 0)
    whole = lambda shape: pl.BlockSpec(
        shape, lambda i, *_: (0,) * len(shape), pipeline_mode=pl.Buffered(1)
    )
    return pl.pallas_call(
        functools.partial(front_kernel, blocks),
        grid_spec=pltpu.PrefetchScalarGridSpec(
            num_scalar_prefetch=0,
            grid=(blocks + groups,),
            in_specs=[
                *[pl.BlockSpec((number,), lambda i: (0,), memory_space=pltpu.SMEM)] * 3,
                pl.BlockSpec((BLOCK, pixels, pixels), lambda i, *_: (at_block(i), 0, 0)),
                whole((2, pixels, pixels)),
                whole((bin_count, rows, pixels)),
                whole((orients, rows)),
                whole((orients, rows)),
            ],
            out_specs=[
                pl.BlockSpec((rows, BLOCK, pixels), lambda i, *_: (0, at_block(i), 0)),
                pl.BlockSpec((1, SLOTS, pixels), lambda i, *_: (at_group(i), 0, 0)),
                pl.BlockSpec((1, SLOTS + orients, pixels), lambda i, *_: (at_group(i), 0, 0)),
                pl.BlockSpec((1, orients, pixels // 2), lambda i, *_: (at_group(i), 0, 0)),
            ],
            scratch_shapes=[
                pltpu.VMEM((classes * orients, rows, pixels), jnp.float32),
                pltpu.VMEM((2, BLOCK * (rows + 8), pixels // 2), jnp.float32),
                pltpu.VMEM((SLOTS, orients * rows), jnp.bfloat16),
                pltpu.VMEM((orients * rows, 2 * pixels), jnp.bfloat16),
                pltpu.VMEM((classes, orients, pixels // 2), jnp.float32),
                pltpu.VMEM((rows, orients), jnp.float32),
            ],
        ),
        out_shape=[
            pltpu.HBM((rows, number, pixels), jnp.bfloat16),
            jax.ShapeDtypeStruct((groups, SLOTS, pixels), jnp.float32),
            jax.ShapeDtypeStruct((groups, SLOTS + orients, pixels), jnp.bfloat16),
            jax.ShapeDtypeStruct((groups, orients, pixels // 2), jnp.float32),
        ],
        compiler_params=pltpu.CompilerParams(vmem_limit_bytes=40 * 2**20),
        cost_estimate=pl.CostEstimate(
            flops=8 * number * pixels**3, bytes_accessed=number * pixels**2 * 4, transcendentals=0
        ),
        name="front",
    )(
        *(
            pltpu.with_memory_space_constraint(x, pltpu.HBM)
            for x in (
                class_ids, orient_ids, bins, images, dft_tables(pixels), ctf_table, slice_slots, slot_weight,
            )
        )
    )


def score_kernel(orients, last, first_ref, sum_ref, w_ref, *refs):
    panels, (out_ref, even, odd) = refs[:-3], refs[-3:]
    step = pl.program_id(0)
    number, pixels = w_ref.shape[1], w_ref.shape[2]

    @pl.when(step == 0)
    def _():
        even[...] = sum_ref[0]
        odd[...] = sum_ref[1]

    if len(panels) == 2:
        blocks = [(ref, c) for ref in panels for c in range(ref.shape[0])]
    else:
        z, core = lax.axis_index("cls") // 2, lax.axis_index("cls") % 2
        groups = range(panels[0].shape[0] // 2)
        blocks = [(panels[0], 2 * (z ^ m) + c) for c in (core, 1 - core) for m in groups]
    totals = [even[...], odd[...]]
    for pair in range(w_ref.shape[0] // 2):
        rows = pl.ds(pair * 2 * orients, 2 * orients)
        both = jnp.concatenate([ref[c, rows, :] for ref, c in blocks], axis=0)
        images = w_ref[2 * pair : 2 * pair + 2].reshape(2 * number, pixels)
        scores = lax.dot_general(
            images, both, (((1,), (1,)), ((), ())), preferred_element_type=jnp.float32
        )
        totals = [totals[0] + scores[:number], totals[1] + scores[number:]]
    even[...], odd[...] = totals

    @pl.when(step == pl.num_programs(0) - 1)
    def _():
        if last is None:
            out_ref[0] = even[...]
            out_ref[1] = odd[...]
        else:
            halves = (-1, 2, orients, number)
            sums = jnp.transpose(even[...]).reshape(halves)[:, 0]
            sums = (sums + jnp.transpose(odd[...]).reshape(halves)[:, 1]) * last
            out_ref[...] = jnp.max(jnp.max(sums, axis=0), axis=0, keepdims=True)


def score(w2, panels, sums, first, last=None, depth=32):
    number, pixels = w2.shape[1], w2.shape[2]
    orients = 8
    steps = panels[0].shape[1] // (depth * orients)
    hbm = lambda x: pltpu.with_memory_space_constraint(x, pltpu.HBM)
    whole = lambda shape: pl.BlockSpec(shape, lambda i, first: (0,) * len(shape))
    out_shape = sums.shape if last is None else (1, number)
    return pl.pallas_call(
        functools.partial(score_kernel, orients, last),
        grid_spec=pltpu.PrefetchScalarGridSpec(
            num_scalar_prefetch=1,
            grid=(steps,),
            in_specs=[
                whole(sums.shape),
                pl.BlockSpec((depth, number, pixels), lambda i, first: (first[0] * steps + i, 0, 0)),
            ]
            + [
                pl.BlockSpec((panel.shape[0], depth * orients, pixels), lambda i, first: (0, i, 0))
                for panel in panels
            ],
            out_specs=whole(out_shape),
            scratch_shapes=[pltpu.VMEM(sums.shape[1:], jnp.float32)] * 2,
        ),
        out_shape=jax.ShapeDtypeStruct(out_shape, jnp.float32),
        compiler_params=pltpu.CompilerParams(vmem_limit_bytes=20 * 2**20),
        name="score",
    )(first[None], sums, hbm(w2), *(hbm(panel) for panel in panels))


def chip_kernel(masks, keep_ref, count_ref, got_ref, own_ref, own_count_ref, *outs):
    size = own_ref.shape[1]
    slots = keep_ref.shape[1]
    lanes = count_ref.shape[2]
    count = count_ref[...] + got_ref[:, pl.ds(slots, 8), pl.ds(0, lanes)].astype(jnp.float32)
    own_count_ref[...] = count

    def part(mask):
        rows = pl.ds(pl.multiple_of((lax.axis_index("img") ^ mask) * size, size), size)
        return keep_ref[:, rows, :] + got_ref[:, rows, :].astype(jnp.float32)

    own_ref[...] = part(0)
    for mask, out_ref in zip(masks, outs, strict=True):
        out_ref[:, pl.ds(0, size), :] = part(mask).astype(jnp.bfloat16)
        tail = count.astype(jnp.bfloat16)
        out_ref[:, pl.ds(size, 8), :] = jnp.concatenate([tail, jnp.zeros_like(tail)], axis=2)


def chip_sum(keep, count, got, imgs):
    groups, slots, pixels = keep.shape
    size = slots // imgs
    masks = tuple(range(1, imgs))
    at = lambda shape: pl.BlockSpec((1, *shape[1:]), lambda i: (i, 0, 0))
    out_shape = [
        jax.ShapeDtypeStruct((groups, size, pixels), jnp.float32),
        jax.ShapeDtypeStruct(count.shape, jnp.float32),
    ] + [jax.ShapeDtypeStruct((groups, size + 8, pixels), jnp.bfloat16)] * (imgs - 1)
    return pl.pallas_call(
        functools.partial(chip_kernel, masks),
        grid=(groups,),
        in_specs=[at(keep.shape), at(count.shape), at(got.shape)],
        out_specs=[at(out.shape) for out in out_shape],
        out_shape=out_shape,
        compiler_params=pltpu.CompilerParams(vmem_limit_bytes=12 * 2**20),
        name="chip_sum",
    )(keep, count, got)


def plane_kernel(masks, own_ref, count_ref, *refs):
    gots, outs = refs[: len(refs) - len(masks) - 2], refs[len(refs) - len(masks) - 2 :]
    data_ref, data_count_ref, sends = outs[0], outs[1], outs[2:]
    size, lanes = own_ref.shape[1], count_ref.shape[2]

    def part(mask):
        z = (lax.axis_index("cls") // 2) ^ mask
        data, count = own_ref[z], count_ref[z]
        for got in gots:
            data = data + got[z, pl.ds(0, size), :].astype(jnp.float32)
            count = count + got[z, pl.ds(size, 8), pl.ds(0, lanes)].astype(jnp.float32)
        return data, count

    data_ref[...], data_count_ref[...] = part(0)
    for mask, send_ref in zip(masks, sends, strict=True):
        data, count = part(mask)
        high = jnp.floor(count * (1.0 / 128.0)) * 128.0
        send_ref[pl.ds(0, size), :] = data.astype(jnp.bfloat16)
        send_ref[pl.ds(size, 8), :] = jnp.concatenate([high, count - high], axis=1).astype(
            jnp.bfloat16
        )


def plane_sum(own, count, gots):
    groups, size, pixels = own.shape
    vmem = pl.BlockSpec()
    masks = tuple(range(1, groups))
    return pl.pallas_call(
        functools.partial(plane_kernel, masks),
        in_specs=[vmem] * (2 + len(gots)),
        out_specs=[vmem] * (groups + 1),
        out_shape=[
            jax.ShapeDtypeStruct((size, pixels), jnp.float32),
            jax.ShapeDtypeStruct(count.shape[1:], jnp.float32),
        ]
        + [jax.ShapeDtypeStruct((size + 8, pixels), jnp.bfloat16)] * (groups - 1),
        compiler_params=pltpu.CompilerParams(vmem_limit_bytes=12 * 2**20),
        name="plane_sum",
    )(own, count, *gots)


def final_kernel(ctf_ref, slot_ref, wt_ref, own_ref, count_ref, *refs):
    gots, (data_ref, weight_ref, squares, scr) = refs[:-4], refs[-4:]
    bin_count, rows, pixels = ctf_ref.shape
    size, orients, lanes = own_ref.shape[0], wt_ref.shape[0], count_ref.shape[1]
    wt_cols = jnp.transpose(wt_ref[...])
    data, count = own_ref[...], count_ref[...]
    for got in gots:
        data = data + got[pl.ds(0, size), :].astype(jnp.float32)
        tail = got[pl.ds(size, 8), :].astype(jnp.float32)
        count = count + (tail[:, :lanes] + tail[:, lanes:])
    data_ref[...] = data
    for b in range(bin_count):
        squares[b] = ctf_ref[b] * ctf_ref[b]
    for o in range(orients):
        value = squares[0] * count[o : o + 1, 0:1]
        for b in range(1, bin_count):
            value = value + squares[b] * count[o : o + 1, b : b + 1]
        value = value * wt_cols[:, o : o + 1]
        for part in range(3):
            piece = value.astype(jnp.bfloat16)
            scr[pl.ds(o * rows, rows), pl.ds(part * pixels, pixels)] = piece
            value = value - piece.astype(jnp.float32)
    target = lax.broadcasted_iota(jnp.int32, (size, rows), 0) + lax.axis_index("img") * size
    hot = jnp.concatenate(
        [
            jnp.where(target == slot_ref[o : o + 1, :], 1.0, 0.0).astype(jnp.bfloat16)
            for o in range(orients)
        ],
        axis=1,
    )
    slab = jnp.dot(hot, scr[...], preferred_element_type=jnp.float32)
    weight_ref[...] = (slab[:, 2 * pixels :] + slab[:, pixels : 2 * pixels]) + slab[:, :pixels]


def final_sum(ctf_table, slice_slots, slot_weight, own, count, gots):
    bin_count, rows, pixels = ctf_table.shape
    orients = slot_weight.shape[0]
    vmem = pl.BlockSpec()
    return pl.pallas_call(
        final_kernel,
        in_specs=[vmem] * (5 + len(gots)),
        out_specs=[vmem, vmem],
        out_shape=[jax.ShapeDtypeStruct(own.shape, jnp.float32)] * 2,
        scratch_shapes=[
            pltpu.VMEM((bin_count, rows, pixels), jnp.float32),
            pltpu.VMEM((orients * rows, 3 * pixels), jnp.bfloat16),
        ],
        compiler_params=pltpu.CompilerParams(vmem_limit_bytes=12 * 2**20),
        name="final_sum",
    )(ctf_table, slice_slots, slot_weight, own, count, *gots)


def swap(value, axis, mask):
    size = lax.axis_size(axis)
    return lax.ppermute(value, axis, [(i, i ^ mask) for i in range(size)])


def on_device(
    images, ctf_table, defocus_bin, projections, best_class, best_orient, slice_slots, slot_weight
):
    classes, imgs = lax.axis_size("cls"), lax.axis_size("img")
    groups = classes // 2
    rows, pixels = ctf_table.shape[1], images.shape[2]
    orients = slot_weight.shape[0]
    near_rows = rows * 1 // 2
    own_panel = jnp.transpose(projections, (0, 2, 1, 3)).reshape(1, -1, pixels)
    cut = near_rows * orients
    my_img = lax.axis_index("img")
    parity = (my_img ^ (my_img >> 1)) & 1
    half = lambda p: lax.dynamic_slice_in_dim(own_panel, p * cut, cut, axis=1)
    near = [swap(half(parity), "cls", 2 * m) for m in range(1, groups)]
    w2, keep, send, count = front(
        images,
        ctf_table,
        best_class.reshape(-1),
        best_orient,
        defocus_bin,
        slice_slots,
        slot_weight,
        classes,
    )
    send, near = lax.optimization_barrier((send, near))
    got = swap(send, "cls", 1)
    own, own_count, *parts = chip_sum(keep, count, got, imgs)
    gots = [swap(part, "img", m + 1) for m, part in enumerate(parts)]
    near = jnp.concatenate([half(parity)] + near, axis=0)
    far = [swap(near[1:, : cut // 2], "img", 1), swap(near[1:, cut // 2 :], "img", 2)]
    other = swap(near, "cls", 1)
    sums = jnp.zeros((2, images.shape[0], 2 * classes * orients), jnp.float32)
    sums = score(w2, [near, other], sums, parity)
    gots, sums, far = lax.optimization_barrier((gots, sums, far))
    data, data_count, *parts = plane_sum(own, own_count, gots)
    gots = [swap(part, "cls", 2 * (m + 1)) for m, part in enumerate(parts)]
    far = jnp.concatenate([half(1 - parity), jnp.concatenate(far, axis=1)], axis=0)
    best = score(w2, [far, swap(far, "cls", 1)], sums, 1 - parity, 1.0 / math.sqrt(rows * pixels))
    gots, best = lax.optimization_barrier((gots, best))
    data, weight = final_sum(ctf_table, slice_slots, slot_weight, data, data_count, gots)
    return (best.reshape(-1), data[None], weight[None])


def solution(mesh):
    return jax.shard_map(
        on_device,
        mesh=mesh,
        in_specs=(
            P(("img", "cls"), None, None),
            P(),
            P(("img", "cls")),
            P("cls", None, None, None),
            P(("img", "cls"), None),
            P(("img", "cls")),
            P(),
            P(),
        ),
        out_specs=(P(("img", "cls")), P("cls", "img", None), P("cls", "img", None)),
        check_vma=False,
    )
```

```python
import functools
import math

import jax
import jax.numpy as jnp
import numpy as np
from jax import lax
from jax.experimental import pallas as pl
from jax.experimental.pallas import tpu as pltpu
from jax.sharding import PartitionSpec as P

SLOTS = 512
BLOCK = 16


def dft_tables(pixels):
    half = pixels // 2
    position = np.arange(pixels)
    norm = 1.0 / math.sqrt(pixels)
    angle_cols = (position[:, None] * np.arange(half)[None, :] % pixels) * (2.0 * math.pi / pixels)
    col_table = np.concatenate([np.cos(angle_cols), -np.sin(angle_cols)], axis=1) * norm
    angle_rows = ((np.arange(half) - half // 2)[:, None] * position[None, :] % pixels) * (
        2.0 * math.pi / pixels
    )
    row_table = np.concatenate([np.cos(angle_rows), np.sin(angle_rows)], axis=0) * norm
    return jnp.asarray(np.stack([col_table, row_table]).astype(np.float32), jnp.bfloat16)


def front_kernel(
    blocks, class_ref, orient_ref, bin_ref, img_ref, table_ref, ctf_ref, slot_ref, wt_ref, w2_ref,
    keep_ref, send_ref, count_ref, acc, wscr, hot, value_scr, counts, wt_scr,
):
    step = pl.program_id(0)
    half = table_ref.shape[1] // 2
    orients, rows = wt_ref.shape
    number = img_ref.shape[0]

    @pl.when(step == 0)
    def _():
        acc[...] = jnp.zeros_like(acc)
        counts[...] = jnp.zeros_like(counts)
        wt_scr[...] = jnp.transpose(wt_ref[...])
        slots = lax.broadcasted_iota(jnp.int32, (hot.shape[0], rows), 0)
        for o in range(orients):
            hot[:, pl.ds(o * rows, rows)] = jnp.where(
                slots == slot_ref[o : o + 1, :], 1.0, 0.0
            ).astype(jnp.bfloat16)

    @pl.when(step < blocks)
    def _():
        lane = lax.broadcasted_iota(jnp.int32, (1, counts.shape[2]), 1)
        for i in range(number):
            one = jnp.dot(img_ref[i], table_ref[0], preferred_element_type=jnp.float32)
            both = jnp.dot(
                table_ref[1], one.astype(jnp.bfloat16), preferred_element_type=jnp.float32
            )
            index = step * number + i
            which_bin = bin_ref[index]
            which_class, which_orient = class_ref[index], orient_ref[index]
            which_pair = which_class * orients + which_orient
            counted = (which_class, pl.ds(which_orient, 1), slice(None))
            counts[counted] += jnp.where(lane == which_bin, 1.0, 0.0)
            real = both[:rows, :half] + both[rows:, half:]
            imag = both[:rows, half:] - both[rows:, :half]
            for part, spec in enumerate((real, imag)):
                lanes = pl.ds(part * half, half)
                weighted = (spec * ctf_ref[which_bin, :, lanes]).astype(jnp.bfloat16)
                weighted = weighted.astype(jnp.float32)
                acc[which_pair, :, lanes] += weighted
                wscr[part, pl.ds(i * (rows + 8), rows), :] = weighted
        for j in range(rows):
            w2_ref[j] = jnp.concatenate(
                [
                    wscr[part, pl.ds(j, number, stride=rows + 8), :]
                    for part in range(2)
                ],
                axis=1,
            ).astype(jnp.bfloat16)

    @pl.when(step >= blocks)
    def _():
        z = step - blocks
        core = lax.axis_index("cls") % 2
        for part, which in enumerate((2 * z + core, 2 * z + 1 - core)):
            for o in range(orients):
                value = acc[which * orients + o] * wt_scr[:, o : o + 1]
                value_scr[pl.ds(o * rows, rows), pl.ds(part * 2 * half, 2 * half)] = value.astype(
                    jnp.bfloat16
                )
        slab = jnp.dot(hot[...], value_scr[...], preferred_element_type=jnp.float32)
        keep_ref[0] = slab[:, : 2 * half]
        send_ref[0, : SLOTS] = slab[:, 2 * half :].astype(jnp.bfloat16)
        send_ref[0, SLOTS :, : half] = counts[2 * z + 1 - core].astype(jnp.bfloat16)
        send_ref[0, SLOTS :, half :] = jnp.zeros((orients, half), jnp.bfloat16)
        count_ref[0] = counts[2 * z + core]


def front(images, ctf_table, class_ids, orient_ids, bins, slice_slots, slot_weight, classes):
    number, pixels = images.shape[0], images.shape[1]
    bin_count, rows = ctf_table.shape[0], ctf_table.shape[1]
    orients = slot_weight.shape[0]
    blocks, groups = number // BLOCK, classes // 2
    at_block = lambda i: jnp.minimum(i, blocks - 1)
    at_group = lambda i: jnp.maximum(i - blocks, 0)
    whole = lambda shape: pl.BlockSpec(
        shape, lambda i, *_: (0,) * len(shape), pipeline_mode=pl.Buffered(1)
    )
    return pl.pallas_call(
        functools.partial(front_kernel, blocks),
        grid_spec=pltpu.PrefetchScalarGridSpec(
            num_scalar_prefetch=0,
            grid=(blocks + groups,),
            in_specs=[
                *[pl.BlockSpec((number,), lambda i: (0,), memory_space=pltpu.SMEM)] * 3,
                pl.BlockSpec((BLOCK, pixels, pixels), lambda i, *_: (at_block(i), 0, 0)),
                whole((2, pixels, pixels)),
                whole((bin_count, rows, pixels)),
                whole((orients, rows)),
                whole((orients, rows)),
            ],
            out_specs=[
                pl.BlockSpec((rows, BLOCK, pixels), lambda i, *_: (0, at_block(i), 0)),
                pl.BlockSpec((1, SLOTS, pixels), lambda i, *_: (at_group(i), 0, 0)),
                pl.BlockSpec((1, SLOTS + orients, pixels), lambda i, *_: (at_group(i), 0, 0)),
                pl.BlockSpec((1, orients, pixels // 2), lambda i, *_: (at_group(i), 0, 0)),
            ],
            scratch_shapes=[
                pltpu.VMEM((classes * orients, rows, pixels), jnp.float32),
                pltpu.VMEM((2, BLOCK * (rows + 8), pixels // 2), jnp.float32),
                pltpu.VMEM((SLOTS, orients * rows), jnp.bfloat16),
                pltpu.VMEM((orients * rows, 2 * pixels), jnp.bfloat16),
                pltpu.VMEM((classes, orients, pixels // 2), jnp.float32),
                pltpu.VMEM((rows, orients), jnp.float32),
            ],
        ),
        out_shape=[
            pltpu.HBM((rows, number, pixels), jnp.bfloat16),
            jax.ShapeDtypeStruct((groups, SLOTS, pixels), jnp.float32),
            jax.ShapeDtypeStruct((groups, SLOTS + orients, pixels), jnp.bfloat16),
            jax.ShapeDtypeStruct((groups, orients, pixels // 2), jnp.float32),
        ],
        compiler_params=pltpu.CompilerParams(vmem_limit_bytes=40 * 2**20),
        cost_estimate=pl.CostEstimate(
            flops=8 * number * pixels**3, bytes_accessed=number * pixels**2 * 4, transcendentals=0
        ),
        name="front",
    )(
        *(
            pltpu.with_memory_space_constraint(x, pltpu.HBM)
            for x in (
                class_ids, orient_ids, bins, images, dft_tables(pixels), ctf_table, slice_slots, slot_weight,
            )
        )
    )


def score_kernel(orients, last, first_ref, sum_ref, w_ref, *refs):
    panels, (out_ref, even, odd) = refs[:-3], refs[-3:]
    step = pl.program_id(0)
    number, pixels = w_ref.shape[1], w_ref.shape[2]

    @pl.when(step == 0)
    def _():
        even[...] = sum_ref[0]
        odd[...] = sum_ref[1]

    if len(panels) == 2:
        blocks = [(ref, c) for ref in panels for c in range(ref.shape[0])]
    else:
        z, core = lax.axis_index("cls") // 2, lax.axis_index("cls") % 2
        groups = range(panels[0].shape[0] // 2)
        blocks = [(panels[0], 2 * (z ^ m) + c) for c in (core, 1 - core) for m in groups]
    totals = [even[...], odd[...]]
    for pair in range(w_ref.shape[0] // 2):
        rows = pl.ds(pair * 2 * orients, 2 * orients)
        both = jnp.concatenate([ref[c, rows, :] for ref, c in blocks], axis=0)
        images = w_ref[2 * pair : 2 * pair + 2].reshape(2 * number, pixels)
        scores = lax.dot_general(
            images, both, (((1,), (1,)), ((), ())), preferred_element_type=jnp.float32
        )
        totals = [totals[0] + scores[:number], totals[1] + scores[number:]]
    even[...], odd[...] = totals

    @pl.when(step == pl.num_programs(0) - 1)
    def _():
        if last is None:
            out_ref[0] = even[...]
            out_ref[1] = odd[...]
        else:
            halves = (-1, 2, orients, number)
            sums = jnp.transpose(even[...]).reshape(halves)[:, 0]
            sums = (sums + jnp.transpose(odd[...]).reshape(halves)[:, 1]) * last
            out_ref[...] = jnp.max(jnp.max(sums, axis=0), axis=0, keepdims=True)


def score(w2, panels, sums, first, last=None, depth=32):
    number, pixels = w2.shape[1], w2.shape[2]
    orients = 8
    steps = panels[0].shape[1] // (depth * orients)
    hbm = lambda x: pltpu.with_memory_space_constraint(x, pltpu.HBM)
    whole = lambda shape: pl.BlockSpec(shape, lambda i, first: (0,) * len(shape))
    out_shape = sums.shape if last is None else (1, number)
    return pl.pallas_call(
        functools.partial(score_kernel, orients, last),
        grid_spec=pltpu.PrefetchScalarGridSpec(
            num_scalar_prefetch=1,
            grid=(steps,),
            in_specs=[
                whole(sums.shape),
                pl.BlockSpec((depth, number, pixels), lambda i, first: (first[0] * steps + i, 0, 0)),
            ]
            + [
                pl.BlockSpec((panel.shape[0], depth * orients, pixels), lambda i, first: (0, i, 0))
                for panel in panels
            ],
            out_specs=whole(out_shape),
            scratch_shapes=[pltpu.VMEM(sums.shape[1:], jnp.float32)] * 2,
        ),
        out_shape=jax.ShapeDtypeStruct(out_shape, jnp.float32),
        compiler_params=pltpu.CompilerParams(vmem_limit_bytes=20 * 2**20),
        name="score",
    )(first[None], sums, hbm(w2), *(hbm(panel) for panel in panels))


def chip_kernel(masks, keep_ref, count_ref, got_ref, own_ref, own_count_ref, *outs):
    size = own_ref.shape[1]
    slots = keep_ref.shape[1]
    lanes = count_ref.shape[2]
    count = count_ref[...] + got_ref[:, pl.ds(slots, 8), pl.ds(0, lanes)].astype(jnp.float32)
    own_count_ref[...] = count

    def part(mask):
        rows = pl.ds(pl.multiple_of((lax.axis_index("img") ^ mask) * size, size), size)
        return keep_ref[:, rows, :] + got_ref[:, rows, :].astype(jnp.float32)

    own_ref[...] = part(0)
    for mask, out_ref in zip(masks, outs, strict=True):
        out_ref[:, pl.ds(0, size), :] = part(mask).astype(jnp.bfloat16)
        tail = count.astype(jnp.bfloat16)
        out_ref[:, pl.ds(size, 8), :] = jnp.concatenate([tail, jnp.zeros_like(tail)], axis=2)


def chip_sum(keep, count, got, imgs):
    groups, slots, pixels = keep.shape
    size = slots // imgs
    masks = tuple(range(1, imgs))
    at = lambda shape: pl.BlockSpec((1, *shape[1:]), lambda i: (i, 0, 0))
    out_shape = [
        jax.ShapeDtypeStruct((groups, size, pixels), jnp.float32),
        jax.ShapeDtypeStruct(count.shape, jnp.float32),
    ] + [jax.ShapeDtypeStruct((groups, size + 8, pixels), jnp.bfloat16)] * (imgs - 1)
    return pl.pallas_call(
        functools.partial(chip_kernel, masks),
        grid=(groups,),
        in_specs=[at(keep.shape), at(count.shape), at(got.shape)],
        out_specs=[at(out.shape) for out in out_shape],
        out_shape=out_shape,
        compiler_params=pltpu.CompilerParams(vmem_limit_bytes=12 * 2**20),
        name="chip_sum",
    )(keep, count, got)


def plane_kernel(masks, own_ref, count_ref, *refs):
    gots, outs = refs[: len(refs) - len(masks) - 2], refs[len(refs) - len(masks) - 2 :]
    data_ref, data_count_ref, sends = outs[0], outs[1], outs[2:]
    size, lanes = own_ref.shape[1], count_ref.shape[2]

    def part(mask):
        z = (lax.axis_index("cls") // 2) ^ mask
        data, count = own_ref[z], count_ref[z]
        for got in gots:
            data = data + got[z, pl.ds(0, size), :].astype(jnp.float32)
            count = count + got[z, pl.ds(size, 8), pl.ds(0, lanes)].astype(jnp.float32)
        return data, count

    data_ref[...], data_count_ref[...] = part(0)
    for mask, send_ref in zip(masks, sends, strict=True):
        data, count = part(mask)
        high = jnp.floor(count * (1.0 / 128.0)) * 128.0
        send_ref[pl.ds(0, size), :] = data.astype(jnp.bfloat16)
        send_ref[pl.ds(size, 8), :] = jnp.concatenate([high, count - high], axis=1).astype(
            jnp.bfloat16
        )


def plane_sum(own, count, gots):
    groups, size, pixels = own.shape
    vmem = pl.BlockSpec()
    masks = tuple(range(1, groups))
    return pl.pallas_call(
        functools.partial(plane_kernel, masks),
        in_specs=[vmem] * (2 + len(gots)),
        out_specs=[vmem] * (groups + 1),
        out_shape=[
            jax.ShapeDtypeStruct((size, pixels), jnp.float32),
            jax.ShapeDtypeStruct(count.shape[1:], jnp.float32),
        ]
        + [jax.ShapeDtypeStruct((size + 8, pixels), jnp.bfloat16)] * (groups - 1),
        compiler_params=pltpu.CompilerParams(vmem_limit_bytes=12 * 2**20),
        name="plane_sum",
    )(own, count, *gots)


def final_kernel(ctf_ref, slot_ref, wt_ref, own_ref, count_ref, *refs):
    gots, (data_ref, weight_ref, squares, scr) = refs[:-4], refs[-4:]
    bin_count, rows, pixels = ctf_ref.shape
    size, orients, lanes = own_ref.shape[0], wt_ref.shape[0], count_ref.shape[1]
    wt_cols = jnp.transpose(wt_ref[...])
    data, count = own_ref[...], count_ref[...]
    for got in gots:
        data = data + got[pl.ds(0, size), :].astype(jnp.float32)
        tail = got[pl.ds(size, 8), :].astype(jnp.float32)
        count = count + (tail[:, :lanes] + tail[:, lanes:])
    data_ref[...] = data
    for b in range(bin_count):
        squares[b] = ctf_ref[b] * ctf_ref[b]
    for o in range(orients):
        value = squares[0] * count[o : o + 1, 0:1]
        for b in range(1, bin_count):
            value = value + squares[b] * count[o : o + 1, b : b + 1]
        value = value * wt_cols[:, o : o + 1]
        for part in range(2):
            piece = value.astype(jnp.bfloat16)
            scr[pl.ds(o * rows, rows), pl.ds(part * pixels, pixels)] = piece
            value = value - piece.astype(jnp.float32)
    target = lax.broadcasted_iota(jnp.int32, (size, rows), 0) + lax.axis_index("img") * size
    hot = jnp.concatenate(
        [
            jnp.where(target == slot_ref[o : o + 1, :], 1.0, 0.0).astype(jnp.bfloat16)
            for o in range(orients)
        ],
        axis=1,
    )
    slab = jnp.dot(hot, scr[...], preferred_element_type=jnp.float32)
    weight_ref[...] = slab[:, pixels:] + slab[:, :pixels]


def final_sum(ctf_table, slice_slots, slot_weight, own, count, gots):
    bin_count, rows, pixels = ctf_table.shape
    orients = slot_weight.shape[0]
    vmem = pl.BlockSpec()
    return pl.pallas_call(
        final_kernel,
        in_specs=[vmem] * (5 + len(gots)),
        out_specs=[vmem, vmem],
        out_shape=[jax.ShapeDtypeStruct(own.shape, jnp.float32)] * 2,
        scratch_shapes=[
            pltpu.VMEM((bin_count, rows, pixels), jnp.float32),
            pltpu.VMEM((orients * rows, 2 * pixels), jnp.bfloat16),
        ],
        compiler_params=pltpu.CompilerParams(vmem_limit_bytes=12 * 2**20),
        name="final_sum",
    )(ctf_table, slice_slots, slot_weight, own, count, *gots)


def swap(value, axis, mask):
    size = lax.axis_size(axis)
    return lax.ppermute(value, axis, [(i, i ^ mask) for i in range(size)])


def on_device(
    images, ctf_table, defocus_bin, projections, best_class, best_orient, slice_slots, slot_weight
):
    classes, imgs = lax.axis_size("cls"), lax.axis_size("img")
    groups = classes // 2
    rows, pixels = ctf_table.shape[1], images.shape[2]
    orients = slot_weight.shape[0]
    near_rows = rows * 1 // 2
    cut = near_rows * orients
    my_img = lax.axis_index("img")
    parity = (my_img ^ (my_img >> 1)) & 1

    def half(p):
        taken = lax.dynamic_slice_in_dim(projections, p * near_rows, near_rows, axis=2)
        return jnp.transpose(taken, (0, 2, 1, 3)).reshape(1, cut, pixels)

    near = [swap(half(parity), "cls", 2 * m) for m in range(1, groups)]
    w2, keep, send, count = front(
        images,
        ctf_table,
        best_class.reshape(-1),
        best_orient,
        defocus_bin,
        slice_slots,
        slot_weight,
        classes,
    )
    send, near = lax.optimization_barrier((send, near))
    got = swap(send, "cls", 1)
    own, own_count, *parts = chip_sum(keep, count, got, imgs)
    gots = [swap(part, "img", m + 1) for m, part in enumerate(parts)]
    near = jnp.concatenate([half(parity)] + near, axis=0)
    far = [swap(near[1:, : cut // 2], "img", 1), swap(near[1:, cut // 2 :], "img", 2)]
    other = swap(near, "cls", 1)
    sums = jnp.zeros((2, images.shape[0], 2 * classes * orients), jnp.float32)
    sums = score(w2, [near, other], sums, parity)
    gots, sums, far = lax.optimization_barrier((gots, sums, far))
    data, data_count, *parts = plane_sum(own, own_count, gots)
    gots = [swap(part, "cls", 2 * (m + 1)) for m, part in enumerate(parts)]
    far = jnp.concatenate([half(1 - parity), jnp.concatenate(far, axis=1)], axis=0)
    best = score(w2, [far, swap(far, "cls", 1)], sums, 1 - parity, 1.0 / math.sqrt(rows * pixels))
    gots, best = lax.optimization_barrier((gots, best))
    data, weight = final_sum(ctf_table, slice_slots, slot_weight, data, data_count, gots)
    return (best.reshape(-1), data[None], weight[None])


def solution(mesh):
    return jax.shard_map(
        on_device,
        mesh=mesh,
        in_specs=(
            P(("img", "cls"), None, None),
            P(),
            P(("img", "cls")),
            P("cls", None, None, None),
            P(("img", "cls"), None),
            P(("img", "cls")),
            P(),
            P(),
        ),
        out_specs=(P(("img", "cls")), P("cls", "img", None), P("cls", "img", None)),
        check_vma=False,
    )
```

```python
import functools
import math

import jax
import jax.numpy as jnp
import numpy as np
from jax import lax
from jax.experimental import pallas as pl
from jax.experimental.pallas import tpu as pltpu
from jax.sharding import PartitionSpec as P

SLOTS = 512
BLOCK = 16


def dft_tables(pixels):
    half = pixels // 2
    position = np.arange(pixels)
    norm = 1.0 / math.sqrt(pixels)
    angle_cols = (position[:, None] * np.arange(half)[None, :] % pixels) * (2.0 * math.pi / pixels)
    col_table = np.concatenate([np.cos(angle_cols), -np.sin(angle_cols)], axis=1) * norm
    angle_rows = ((np.arange(half) - half // 2)[:, None] * position[None, :] % pixels) * (
        2.0 * math.pi / pixels
    )
    row_table = np.concatenate([np.cos(angle_rows), np.sin(angle_rows)], axis=0) * norm
    return jnp.asarray(np.stack([col_table, row_table]).astype(np.float32), jnp.bfloat16)


def front_kernel(
    blocks, class_ref, orient_ref, bin_ref, img_ref, table_ref, ctf_ref, slot_ref, wt_ref, w2_ref,
    keep_ref, send_ref, count_ref, acc, wscr, hot, value_scr, counts, wt_scr,
):
    step = pl.program_id(0)
    half = table_ref.shape[1] // 2
    orients, rows = wt_ref.shape
    number = img_ref.shape[0]

    @pl.when(step == 0)
    def _():
        acc[...] = jnp.zeros_like(acc)
        counts[...] = jnp.zeros_like(counts)
        wt_scr[...] = jnp.transpose(wt_ref[...])
        slots = lax.broadcasted_iota(jnp.int32, (hot.shape[0], rows), 0)
        for o in range(orients):
            hot[:, pl.ds(o * rows, rows)] = jnp.where(
                slots == slot_ref[o : o + 1, :], 1.0, 0.0
            ).astype(jnp.bfloat16)

    @pl.when(step < blocks)
    def _():
        lane = lax.broadcasted_iota(jnp.int32, (1, counts.shape[2]), 1)
        for i in range(number):
            one = jnp.dot(img_ref[i], table_ref[0], preferred_element_type=jnp.float32)
            both = jnp.dot(
                table_ref[1], one.astype(jnp.bfloat16), preferred_element_type=jnp.float32
            )
            index = step * number + i
            which_bin = bin_ref[index]
            which_class, which_orient = class_ref[index], orient_ref[index]
            which_pair = which_class * orients + which_orient
            counted = (which_class, pl.ds(which_orient, 1), slice(None))
            counts[counted] += jnp.where(lane == which_bin, 1.0, 0.0)
            real = both[:rows, :half] + both[rows:, half:]
            imag = both[:rows, half:] - both[rows:, :half]
            for part, spec in enumerate((real, imag)):
                lanes = pl.ds(part * half, half)
                weighted = (spec * ctf_ref[which_bin, :, lanes]).astype(jnp.bfloat16)
                weighted = weighted.astype(jnp.float32)
                acc[which_pair, :, lanes] += weighted
                wscr[part, pl.ds(i * (rows + 8), rows), :] = weighted
        for j in range(rows):
            w2_ref[j] = jnp.concatenate(
                [
                    wscr[part, pl.ds(j, number, stride=rows + 8), :]
                    for part in range(2)
                ],
                axis=1,
            ).astype(jnp.bfloat16)

    @pl.when(step >= blocks)
    def _():
        z = step - blocks
        core = lax.axis_index("cls") % 2
        for part, which in enumerate((2 * z + core, 2 * z + 1 - core)):
            for o in range(orients):
                value = acc[which * orients + o] * wt_scr[:, o : o + 1]
                value_scr[pl.ds(o * rows, rows), pl.ds(part * 2 * half, 2 * half)] = value.astype(
                    jnp.bfloat16
                )
        slab = jnp.dot(hot[...], value_scr[...], preferred_element_type=jnp.float32)
        keep_ref[0] = slab[:, : 2 * half]
        send_ref[0, : SLOTS] = slab[:, 2 * half :].astype(jnp.bfloat16)
        send_ref[0, SLOTS :, : half] = counts[2 * z + 1 - core].astype(jnp.bfloat16)
        send_ref[0, SLOTS :, half :] = jnp.zeros((orients, half), jnp.bfloat16)
        count_ref[0] = counts[2 * z + core]


def front(images, ctf_table, class_ids, orient_ids, bins, slice_slots, slot_weight, classes):
    number, pixels = images.shape[0], images.shape[1]
    bin_count, rows = ctf_table.shape[0], ctf_table.shape[1]
    orients = slot_weight.shape[0]
    blocks, groups = number // BLOCK, classes // 2
    at_block = lambda i: jnp.minimum(i, blocks - 1)
    at_group = lambda i: jnp.maximum(i - blocks, 0)
    whole = lambda shape: pl.BlockSpec(
        shape, lambda i, *_: (0,) * len(shape), pipeline_mode=pl.Buffered(1)
    )
    return pl.pallas_call(
        functools.partial(front_kernel, blocks),
        grid_spec=pltpu.PrefetchScalarGridSpec(
            num_scalar_prefetch=0,
            grid=(blocks + groups,),
            in_specs=[
                *[pl.BlockSpec((number,), lambda i: (0,), memory_space=pltpu.SMEM)] * 3,
                pl.BlockSpec((BLOCK, pixels, pixels), lambda i, *_: (at_block(i), 0, 0)),
                whole((2, pixels, pixels)),
                whole((bin_count, rows, pixels)),
                whole((orients, rows)),
                whole((orients, rows)),
            ],
            out_specs=[
                pl.BlockSpec((rows, BLOCK, pixels), lambda i, *_: (0, at_block(i), 0)),
                pl.BlockSpec((1, SLOTS, pixels), lambda i, *_: (at_group(i), 0, 0)),
                pl.BlockSpec((1, SLOTS + orients, pixels), lambda i, *_: (at_group(i), 0, 0)),
                pl.BlockSpec((1, orients, pixels // 2), lambda i, *_: (at_group(i), 0, 0)),
            ],
            scratch_shapes=[
                pltpu.VMEM((classes * orients, rows, pixels), jnp.float32),
                pltpu.VMEM((2, BLOCK * (rows + 8), pixels // 2), jnp.float32),
                pltpu.VMEM((SLOTS, orients * rows), jnp.bfloat16),
                pltpu.VMEM((orients * rows, 2 * pixels), jnp.bfloat16),
                pltpu.VMEM((classes, orients, pixels // 2), jnp.float32),
                pltpu.VMEM((rows, orients), jnp.float32),
            ],
        ),
        out_shape=[
            pltpu.HBM((rows, number, pixels), jnp.bfloat16),
            jax.ShapeDtypeStruct((groups, SLOTS, pixels), jnp.float32),
            jax.ShapeDtypeStruct((groups, SLOTS + orients, pixels), jnp.bfloat16),
            jax.ShapeDtypeStruct((groups, orients, pixels // 2), jnp.float32),
        ],
        compiler_params=pltpu.CompilerParams(vmem_limit_bytes=40 * 2**20),
        cost_estimate=pl.CostEstimate(
            flops=8 * number * pixels**3, bytes_accessed=number * pixels**2 * 4, transcendentals=0
        ),
        name="front",
    )(
        *(
            pltpu.with_memory_space_constraint(x, pltpu.HBM)
            for x in (
                class_ids, orient_ids, bins, images, dft_tables(pixels), ctf_table, slice_slots, slot_weight,
            )
        )
    )


def score_kernel(orients, last, first_ref, sum_ref, w_ref, *refs):
    panels, (out_ref, even, odd) = refs[:-3], refs[-3:]
    step = pl.program_id(0)
    number, pixels = w_ref.shape[1], w_ref.shape[2]

    @pl.when(step == 0)
    def _():
        even[...] = sum_ref[0]
        odd[...] = sum_ref[1]

    if len(panels) == 2:
        blocks = [(ref, c) for ref in panels for c in range(ref.shape[0])]
    else:
        z, core = lax.axis_index("cls") // 2, lax.axis_index("cls") % 2
        groups = range(panels[0].shape[0] // 2)
        blocks = [(panels[0], 2 * (z ^ m) + c) for c in (core, 1 - core) for m in groups]
    totals = [even[...], odd[...]]
    for pair in range(w_ref.shape[0] // 2):
        rows = pl.ds(pair * 2 * orients, 2 * orients)
        both = jnp.concatenate([ref[c, rows, :] for ref, c in blocks], axis=0)
        images = w_ref[2 * pair : 2 * pair + 2].reshape(2 * number, pixels)
        scores = lax.dot_general(
            images, both, (((1,), (1,)), ((), ())), preferred_element_type=jnp.float32
        )
        totals = [totals[0] + scores[:number], totals[1] + scores[number:]]
    even[...], odd[...] = totals

    @pl.when(step == pl.num_programs(0) - 1)
    def _():
        if last is None:
            out_ref[0] = even[...]
            out_ref[1] = odd[...]
        else:
            halves = (-1, 2, orients, number)
            sums = jnp.transpose(even[...]).reshape(halves)[:, 0]
            sums = (sums + jnp.transpose(odd[...]).reshape(halves)[:, 1]) * last
            out_ref[...] = jnp.max(jnp.max(sums, axis=0), axis=0, keepdims=True)


def score(w2, panels, sums, first, last=None, depth=32):
    number, pixels = w2.shape[1], w2.shape[2]
    orients = 8
    steps = panels[0].shape[1] // (depth * orients)
    hbm = lambda x: pltpu.with_memory_space_constraint(x, pltpu.HBM)
    whole = lambda shape: pl.BlockSpec(shape, lambda i, first: (0,) * len(shape))
    out_shape = sums.shape if last is None else (1, number)
    return pl.pallas_call(
        functools.partial(score_kernel, orients, last),
        grid_spec=pltpu.PrefetchScalarGridSpec(
            num_scalar_prefetch=1,
            grid=(steps,),
            in_specs=[
                whole(sums.shape),
                pl.BlockSpec((depth, number, pixels), lambda i, first: (first[0] * steps + i, 0, 0)),
            ]
            + [
                pl.BlockSpec((panel.shape[0], depth * orients, pixels), lambda i, first: (0, i, 0))
                for panel in panels
            ],
            out_specs=whole(out_shape),
            scratch_shapes=[pltpu.VMEM(sums.shape[1:], jnp.float32)] * 2,
        ),
        out_shape=jax.ShapeDtypeStruct(out_shape, jnp.float32),
        compiler_params=pltpu.CompilerParams(vmem_limit_bytes=20 * 2**20),
        name="score",
    )(first[None], sums, hbm(w2), *(hbm(panel) for panel in panels))


def chip_kernel(masks, keep_ref, count_ref, got_ref, own_ref, own_count_ref, *outs):
    size = own_ref.shape[1]
    slots = keep_ref.shape[1]
    lanes = count_ref.shape[2]
    count = count_ref[...] + got_ref[:, pl.ds(slots, 8), pl.ds(0, lanes)].astype(jnp.float32)
    own_count_ref[...] = count

    def part(mask):
        rows = pl.ds(pl.multiple_of((lax.axis_index("img") ^ mask) * size, size), size)
        return keep_ref[:, rows, :] + got_ref[:, rows, :].astype(jnp.float32)

    own_ref[...] = part(0)
    for mask, out_ref in zip(masks, outs, strict=True):
        out_ref[:, pl.ds(0, size), :] = part(mask).astype(jnp.bfloat16)
        tail = count.astype(jnp.bfloat16)
        out_ref[:, pl.ds(size, 8), :] = jnp.concatenate([tail, jnp.zeros_like(tail)], axis=2)


def chip_sum(keep, count, got, imgs):
    groups, slots, pixels = keep.shape
    size = slots // imgs
    masks = tuple(range(1, imgs))
    at = lambda shape: pl.BlockSpec((1, *shape[1:]), lambda i: (i, 0, 0))
    out_shape = [
        jax.ShapeDtypeStruct((groups, size, pixels), jnp.float32),
        jax.ShapeDtypeStruct(count.shape, jnp.float32),
    ] + [jax.ShapeDtypeStruct((groups, size + 8, pixels), jnp.bfloat16)] * (imgs - 1)
    return pl.pallas_call(
        functools.partial(chip_kernel, masks),
        grid=(groups,),
        in_specs=[at(keep.shape), at(count.shape), at(got.shape)],
        out_specs=[at(out.shape) for out in out_shape],
        out_shape=out_shape,
        compiler_params=pltpu.CompilerParams(vmem_limit_bytes=12 * 2**20),
        name="chip_sum",
    )(keep, count, got)


def plane_kernel(masks, own_ref, count_ref, *refs):
    gots, outs = refs[: len(refs) - len(masks) - 2], refs[len(refs) - len(masks) - 2 :]
    data_ref, data_count_ref, sends = outs[0], outs[1], outs[2:]
    size, lanes = own_ref.shape[1], count_ref.shape[2]

    def part(mask):
        z = (lax.axis_index("cls") // 2) ^ mask
        data, count = own_ref[z], count_ref[z]
        for got in gots:
            data = data + got[z, pl.ds(0, size), :].astype(jnp.float32)
            count = count + got[z, pl.ds(size, 8), pl.ds(0, lanes)].astype(jnp.float32)
        return data, count

    data_ref[...], data_count_ref[...] = part(0)
    for mask, send_ref in zip(masks, sends, strict=True):
        data, count = part(mask)
        high = jnp.floor(count * (1.0 / 128.0)) * 128.0
        send_ref[pl.ds(0, size), :] = data.astype(jnp.bfloat16)
        send_ref[pl.ds(size, 8), :] = jnp.concatenate([high, count - high], axis=1).astype(
            jnp.bfloat16
        )


def plane_sum(own, count, gots):
    groups, size, pixels = own.shape
    vmem = pl.BlockSpec()
    masks = tuple(range(1, groups))
    return pl.pallas_call(
        functools.partial(plane_kernel, masks),
        in_specs=[vmem] * (2 + len(gots)),
        out_specs=[vmem] * (groups + 1),
        out_shape=[
            jax.ShapeDtypeStruct((size, pixels), jnp.float32),
            jax.ShapeDtypeStruct(count.shape[1:], jnp.float32),
        ]
        + [jax.ShapeDtypeStruct((size + 8, pixels), jnp.bfloat16)] * (groups - 1),
        compiler_params=pltpu.CompilerParams(vmem_limit_bytes=12 * 2**20),
        name="plane_sum",
    )(own, count, *gots)


def final_kernel(ctf_ref, slot_ref, wt_ref, own_ref, count_ref, *refs):
    gots, (data_ref, weight_ref, squares, scr) = refs[:-4], refs[-4:]
    bin_count, rows, pixels = ctf_ref.shape
    size, orients, lanes = own_ref.shape[0], wt_ref.shape[0], count_ref.shape[1]
    wt_cols = jnp.transpose(wt_ref[...])
    data, count = own_ref[...], count_ref[...]
    for got in gots:
        data = data + got[pl.ds(0, size), :].astype(jnp.float32)
        tail = got[pl.ds(size, 8), :].astype(jnp.float32)
        count = count + (tail[:, :lanes] + tail[:, lanes:])
    data_ref[...] = data
    for b in range(bin_count):
        squares[b] = ctf_ref[b] * ctf_ref[b]
    for o in range(orients):
        value = squares[0] * count[o : o + 1, 0:1]
        for b in range(1, bin_count):
            value = value + squares[b] * count[o : o + 1, b : b + 1]
        value = value * wt_cols[:, o : o + 1]
        for part in range(2):
            piece = value.astype(jnp.bfloat16)
            scr[pl.ds(o * rows, rows), pl.ds(part * pixels, pixels)] = piece
            value = value - piece.astype(jnp.float32)
    target = lax.broadcasted_iota(jnp.int32, (size, rows), 0) + lax.axis_index("img") * size
    hot = jnp.concatenate(
        [
            jnp.where(target == slot_ref[o : o + 1, :], 1.0, 0.0).astype(jnp.bfloat16)
            for o in range(orients)
        ],
        axis=1,
    )
    slab = jnp.dot(hot, scr[...], preferred_element_type=jnp.float32)
    weight_ref[...] = slab[:, pixels:] + slab[:, :pixels]


def final_sum(ctf_table, slice_slots, slot_weight, own, count, gots):
    bin_count, rows, pixels = ctf_table.shape
    orients = slot_weight.shape[0]
    vmem = pl.BlockSpec()
    return pl.pallas_call(
        final_kernel,
        in_specs=[vmem] * (5 + len(gots)),
        out_specs=[vmem, vmem],
        out_shape=[jax.ShapeDtypeStruct(own.shape, jnp.float32)] * 2,
        scratch_shapes=[
            pltpu.VMEM((bin_count, rows, pixels), jnp.float32),
            pltpu.VMEM((orients * rows, 2 * pixels), jnp.bfloat16),
        ],
        compiler_params=pltpu.CompilerParams(vmem_limit_bytes=12 * 2**20),
        name="final_sum",
    )(ctf_table, slice_slots, slot_weight, own, count, *gots)


def swap(value, axis, mask):
    size = lax.axis_size(axis)
    return lax.ppermute(value, axis, [(i, i ^ mask) for i in range(size)])


def on_device(
    images, ctf_table, defocus_bin, projections, best_class, best_orient, slice_slots, slot_weight
):
    classes, imgs = lax.axis_size("cls"), lax.axis_size("img")
    groups = classes // 2
    rows, pixels = ctf_table.shape[1], images.shape[2]
    orients = slot_weight.shape[0]
    near_rows = rows * 1 // 2
    cut = near_rows * orients
    my_img = lax.axis_index("img")
    parity = (my_img ^ (my_img >> 1)) & 1

    def half(p):
        taken = lax.dynamic_slice_in_dim(projections, p * near_rows, near_rows, axis=2)
        return jnp.transpose(taken, (0, 2, 1, 3)).reshape(1, cut, pixels)

    near = [swap(half(parity), "cls", 2 * m) for m in range(1, groups)]
    w2, keep, send, count = front(
        images,
        ctf_table,
        best_class.reshape(-1),
        best_orient,
        defocus_bin,
        slice_slots,
        slot_weight,
        classes,
    )
    send, near = lax.optimization_barrier((send, near))
    got = swap(send, "cls", 1)
    own, own_count, *parts = chip_sum(keep, count, got, imgs)
    gots = [swap(part, "img", m + 1) for m, part in enumerate(parts)]
    near = jnp.concatenate([half(parity)] + near, axis=0)
    far = [swap(near[1:, : cut // 2], "img", 1), swap(near[1:, cut // 2 :], "img", 2)]
    _, later = lax.optimization_barrier((own_count, near))
    other = swap(later, "cls", 1)
    sums = jnp.zeros((2, images.shape[0], 2 * classes * orients), jnp.float32)
    sums = score(w2, [near, other], sums, parity)
    gots, sums, far = lax.optimization_barrier((gots, sums, far))
    data, data_count, *parts = plane_sum(own, own_count, gots)
    gots = [swap(part, "cls", 2 * (m + 1)) for m, part in enumerate(parts)]
    far = jnp.concatenate([half(1 - parity), jnp.concatenate(far, axis=1)], axis=0)
    best = score(w2, [far, swap(far, "cls", 1)], sums, 1 - parity, 1.0 / math.sqrt(rows * pixels))
    gots, best = lax.optimization_barrier((gots, best))
    data, weight = final_sum(ctf_table, slice_slots, slot_weight, data, data_count, gots)
    return (best.reshape(-1), data[None], weight[None])


def solution(mesh):
    return jax.shard_map(
        on_device,
        mesh=mesh,
        in_specs=(
            P(("img", "cls"), None, None),
            P(),
            P(("img", "cls")),
            P("cls", None, None, None),
            P(("img", "cls"), None),
            P(("img", "cls")),
            P(),
            P(),
        ),
        out_specs=(P(("img", "cls")), P("cls", "img", None), P("cls", "img", None)),
        check_vma=False,
    )
```
